32 devices in a mesh: ny: 4 (over x, core), nx: 8 (over z, y).
Axes of the slice: x: 2, y: 2, z: 4, core: 2. Of those that a mesh axis runs over, the one named last changes fastest.
Arguments:
- elevation: float32 [576, 9216], P('ny', 'nx'), may hold values from -6 to 6
- flux_x: float32 [576, 9216], P('ny', 'nx'), may hold values from -3 to 3
- flux_y: float32 [576, 9216], P('ny', 'nx'), may hold values from -3 to 3
- depth: float32 [576, 9216], P('ny', 'nx'), may hold values from 0.5 to 2
- wet_mask: int32 [4, 576, 9216], P(None, 'ny', 'nx'), may hold values 0 or 1
- shifts: int32 [4, 2], replicated, may hold values from 0 to 9, as said below
- parent_vals: float32 [4, 8192, 128], P(None, ('ny', 'nx')), may hold values from -3 to 3
- row_dest: int32 [4, 8192], P(None, ('ny', 'nx')), may hold values from 0 to 31, as said below
- row_coarse: int32 [4, 8192], P(None, ('ny', 'nx')), may hold values from 0 to 15
- edge_owner: int32 [4, 4], P(None, 'ny'), may hold values from 0 to 7
- edge_panels: float32 [4, 8, 576], P(None, 'nx', 'ny'), may hold values from -8 to 8
Outputs:
- elevation_out: float32 [576, 9216], P('ny', 'nx')
- flux_x_out: float32 [576, 9216], P('ny', 'nx')
- flux_y_out: float32 [576, 9216], P('ny', 'nx')
The draws below stay inside these ranges and needn't reach their ends.
Inputs may be any that keep to these rules, and one draw needn't show every extreme that they name: In every draw some step shifts the rows by 9 and some step shifts the columns by 9. `row_dest`: in each step, of the 256 rows of one device at most 8 name any one owner; in each step one owner is named by exactly 8 rows of every device.
All inputs are finite; a program needn't handle non-finite values. No bound on the sum of `wet_mask` on one device may be relied on, other than what follows from the above.
Results may differ from the reference program's by a relative error of at most 0.00014.
Values sent between devices are 32-bit elements; how exact they have to be, the bound alone decides.
A program may use at most 128 MiB of HBM per device.

```python
import math
import jax
import jax.numpy as jnp
from jax import lax

RATIO = 9
CYC = 16
PW = 128
STEPS = 4
SH = 9
PR_DEV = 256
CAP = 8
CY = 144
CX = 1152
NYG = 576
NXG = 9216
OWNERS = 32
PRT = 8192
N_NY = 4
N_NX = 8


def draw_shifts(key, part):
    first_key, row_key, col_key = jax.random.split(key, 3)
    base_shifts = jax.random.randint(first_key, (STEPS, 2), 0, SH + 1).astype(jnp.int32)
    row_step = jax.random.randint(row_key, (), 0, STEPS)
    col_step = jax.random.randint(col_key, (), 0, STEPS)
    base_shifts = base_shifts.at[row_step, 0].set(SH)
    return base_shifts.at[col_step, 1].set(SH).astype(jnp.int32)


def draw_row_dest(key, part):
    star_key, block_key = jax.random.split(key)
    stars = jax.random.randint(star_key, (STEPS,), 0, OWNERS).astype(jnp.int32)

    def one_block(block_seed, star_owner):
        pick_key, order_key = jax.random.split(block_seed)
        picked = jax.random.permutation(pick_key, (OWNERS - 1) * CAP)[:PR_DEV - CAP].astype(jnp.int32)
        other_owners = picked // CAP
        other_owners = other_owners + (other_owners >= star_owner).astype(jnp.int32)
        full_rows = jnp.zeros((CAP,), jnp.int32) + star_owner
        all_rows = jnp.concatenate([full_rows, other_owners.astype(jnp.int32)])
        return jax.random.permutation(order_key, all_rows)
    block_seeds = jax.random.split(block_key, STEPS * OWNERS)
    star_rows = jnp.repeat(stars, OWNERS)
    drawn = jax.vmap(one_block)(block_seeds, star_rows)
    return drawn.reshape(STEPS, OWNERS * PR_DEV).astype(jnp.int32)


def set_ends(values, own_key, low, high):
    place = [jax.random.randint(jax.random.fold_in(own_key, axis), (), 0, length) for axis, length in enumerate(values.shape)]
    longest = values.shape.index(max(values.shape))
    neighbour = place[:longest] + [(place[longest] + 1) % values.shape[longest]] + place[longest + 1:]
    return values.at[tuple(place)].set(low).at[tuple(neighbour)].set(high)


def block_levels(stream_key, dims, pieces, low, high):
    factor_of, own = 1.0, jax.random.fold_in(stream_key, 6)
    for axis_at, shards_of in pieces:
        draws = jnp.exp(jax.random.uniform(jax.random.fold_in(own, axis_at), (shards_of,), jnp.float32, low / len(pieces), high / len(pieces)))
        factor_of = factor_of * jnp.repeat(draws, dims[axis_at] // shards_of).reshape([-1 if axis == axis_at else 1 for axis in range(len(dims))])
    return factor_of


def centred(key, extent, scale, most, shards=(), kind=jnp.bfloat16):
    array = scale * jax.random.normal(key, extent, jnp.float32)
    if shards:
        array = array * block_levels(key, extent, shards, -0.22, 0.18)
    return jnp.clip(array, -most, most).astype(kind)


def setup_inputs(seed: int = 0) -> dict:
    arg_keys = jax.random.split(jax.random.key(seed), 12)
    elevation = centred(arg_keys[0], (NYG, NXG), 1.0, 6.0, ((0, 4), (1, 8)), jnp.float32)
    flux_x = centred(arg_keys[1], (NYG, NXG), 0.5, 3.0, ((0, 4), (1, 8)), jnp.float32)
    flux_y = centred(arg_keys[2], (NYG, NXG), 0.5, 3.0, ((0, 4), (1, 8)), jnp.float32)
    depth = jnp.clip(jnp.exp(math.log(2.0) - 1.3862944 * jax.random.uniform(arg_keys[3], (NYG, NXG), jnp.float32) ** block_levels(arg_keys[3], (NYG, NXG), ((0, 4), (1, 8)), -0.2, 0.2)), 0.5, 2.0)
    wet_mask = set_ends((jax.random.randint(arg_keys[4], (STEPS, NYG, NXG), 0, 5) < 4).astype(jnp.int32), jax.random.fold_in(arg_keys[4], 1), 0, 1)
    shifts = draw_shifts(jax.random.fold_in(arg_keys[11], 71), 0)
    parent_vals = centred(arg_keys[6], (STEPS, PRT, PW), 0.5, 3.0, ((1, 32),), jnp.float32)
    row_dest = draw_row_dest(jax.random.fold_in(arg_keys[11], 71), 0)
    row_coarse = set_ends(jax.random.randint(arg_keys[8], (STEPS, PRT), 0, CYC), jax.random.fold_in(arg_keys[8], 1), 0, CYC - 1).astype(jnp.int32)
    edge_owner = set_ends(jax.random.randint(arg_keys[9], (STEPS, N_NY), 0, N_NX), jax.random.fold_in(arg_keys[9], 1), 0, N_NX - 1).astype(jnp.int32)
    edge_panels = centred(arg_keys[10], (STEPS, N_NX, NYG), 2.0, 8.0, ((1, 8), (2, 4)), jnp.float32)
    return dict(elevation=elevation, flux_x=flux_x, flux_y=flux_y, depth=depth, wet_mask=wet_mask, shifts=shifts, parent_vals=parent_vals, row_dest=row_dest, row_coarse=row_coarse, edge_owner=edge_owner, edge_panels=edge_panels)


diffuse = 0.25
step_gain = 0.25


def interp_matrix(fine_count, coarse_count):
    fine_index = jnp.arange(fine_count, dtype=jnp.int32)
    numerator = 2 * fine_index + 1 - RATIO
    lower_index = jnp.clip(numerator // (2 * RATIO), 0, coarse_count - 2)
    weight = jnp.clip((numerator - lower_index * 2 * RATIO).astype(jnp.float32) / (2.0 * RATIO), 0.0, 1.0)
    coarse_index = jnp.arange(coarse_count, dtype=jnp.int32)
    at_lower = jnp.where(coarse_index[None, :] == lower_index[:, None], 1.0 - weight[:, None], 0.0)
    at_upper = jnp.where(coarse_index[None, :] == lower_index[:, None] + 1, weight[:, None], 0.0)
    return at_lower + at_upper


def west_of(grid_field):
    return grid_field[1:-1, :-1]


def east_of(grid_field):
    return grid_field[1:-1, 1:]


def south_of(grid_field):
    return grid_field[:-1, 1:-1]


def north_of(grid_field):
    return grid_field[1:, 1:-1]


def change(across, along):
    return across[:, 1:] - across[:, :-1] + along[1:, :] - along[:-1, :]


def advance(padded, depth_pad):
    surface, flow_x, flow_y, wetness = padded[0], padded[1], padded[2], padded[3]
    open_x = west_of(wetness) * east_of(wetness)
    mass_x = open_x * (0.5 * (west_of(flow_x) + east_of(flow_x)) - diffuse * (east_of(surface) - west_of(surface)))
    push_x = open_x * (0.25 * (west_of(depth_pad) + east_of(depth_pad)) * (west_of(surface) + east_of(surface)) - diffuse * (east_of(flow_x) - west_of(flow_x)))
    shear_x = open_x * (-diffuse * (east_of(flow_y) - west_of(flow_y)))
    open_y = south_of(wetness) * north_of(wetness)
    mass_y = open_y * (0.5 * (south_of(flow_y) + north_of(flow_y)) - diffuse * (north_of(surface) - south_of(surface)))
    push_y = open_y * (0.25 * (south_of(depth_pad) + north_of(depth_pad)) * (south_of(surface) + north_of(surface)) - diffuse * (north_of(flow_y) - south_of(flow_y)))
    shear_y = open_y * (-diffuse * (north_of(flow_x) - south_of(flow_x)))
    inner = wetness[1:-1, 1:-1]
    new_surface = surface[1:-1, 1:-1] - step_gain * change(mass_x, mass_y)
    new_flow_x = inner * (flow_x[1:-1, 1:-1] - step_gain * change(push_x, shear_y))
    new_flow_y = inner * (flow_y[1:-1, 1:-1] - step_gain * change(shear_x, push_y))
    return new_surface, new_flow_x, new_flow_y


def reference(elevation, flux_x, flux_y, depth, wet_mask, shifts, parent_vals, row_dest, row_coarse, edge_owner, edge_panels):
    rows_interp = interp_matrix(CY, CYC)
    cols_interp = interp_matrix(CX, PW)
    current = jnp.stack([elevation, flux_x, flux_y])
    depth_pad = jnp.pad(depth, 1)
    blocks = jnp.arange(N_NY, dtype=jnp.int32)
    for step_index in range(STEPS):
        widened = jnp.pad(current, ((0, 0), (0, SH), (0, SH)))
        shifted = lax.dynamic_slice(widened, (jnp.zeros((), jnp.int32), shifts[step_index, 0], shifts[step_index, 1]), (3, NYG, NXG))
        segment_ids = (row_dest[step_index] * CYC + row_coarse[step_index]).astype(jnp.int32)
        forcing_coarse = jax.ops.segment_sum(parent_vals[step_index], segment_ids, num_segments=OWNERS * CYC)
        forcing_coarse = forcing_coarse.reshape(N_NY, N_NX, CYC, PW)
        row_section = jnp.einsum("ic,abcp->aibp", rows_interp, forcing_coarse, precision=lax.Precision.HIGHEST)
        fine_forcing = jnp.einsum("aibp,jp->aibj", row_section, cols_interp, precision=lax.Precision.HIGHEST).reshape(NYG, NXG)
        raised = shifted[0] + fine_forcing
        edge_values = edge_panels[step_index].reshape(N_NX, N_NY, CY)[edge_owner[step_index], blocks].reshape(NYG)
        stacked = jnp.stack([raised, shifted[1], shifted[2], wet_mask[step_index].astype(jnp.float32)])
        padded = jnp.pad(stacked, ((0, 0), (1, 1), (1, 1)))
        padded = padded.at[0, 1:-1, 0].set(edge_values).at[3, 1:-1, 0].set(1.0)
        current = jnp.stack(advance(padded, depth_pad))
    return current[0], current[1], current[2]
```

```python
import functools

import jax
import jax.numpy as jnp
from jax import lax
from jax.experimental import pallas as pl
from jax.experimental.pallas import tpu as pltpu
from jax.sharding import PartitionSpec as P

RATIO = 9
STEPS = 4
SH = 9
CAP = 8
PAD = 8
LANES = 128
MESH = pl.DeviceIdType.MESH
F32 = jnp.float32
BF16 = jnp.bfloat16
I32 = jnp.int32

STATE_HI = STEPS * (SH + 1)
WET_HI = [SH * (STEPS - 1 - s) + STEPS - s for s in range(STEPS)]
WET_LO = [STEPS - s for s in range(STEPS)]
AUX_HI = [WET_HI[0]] + WET_HI
AUX_LO = [WET_LO[0]] + WET_LO


def starts(widths):
    return [sum(widths[:k]) for k in range(len(widths))]


def round_up(value, unit):
    return -(-value // unit) * unit


def pieces(value):
    high = value.astype(BF16)
    rest = value - high.astype(F32)
    mid = rest.astype(BF16)
    low = (rest - mid.astype(F32)).astype(BF16)
    return high, mid, low


def iota(shape, dim):
    return lax.broadcasted_iota(I32, shape, dim)


def prep_kernel(owners, dest, coarse, vals, e, u, v, d_0, d_1, w_0, w_1, eowner, epanel,
                send, tgt, hi, lo, edge):
    depth, wet = (d_0, d_1), (w_0, w_1)
    rows = dest.shape[1]
    places = owners * CAP
    before = (iota((rows, rows), 0) < iota((rows, rows), 1)).astype(BF16)
    targets = jnp.zeros((owners, LANES), F32)
    for s in range(STEPS):
        d = dest[s : s + 1, :]
        hits = iota((owners, rows), 0) == d
        hits_f = hits.astype(F32)
        earlier = jnp.dot(hits.astype(BF16), before, preferred_element_type=F32)
        rank = jnp.sum(hits_f * earlier, axis=0, keepdims=True).astype(I32)
        place = d * CAP + rank
        pick = (iota((places, rows), 0) == place).astype(BF16)
        total = jnp.zeros((places, vals.shape[2]), F32)
        for piece in pieces(vals[s]):
            total = total + jnp.dot(pick, piece, preferred_element_type=F32)
        send[:, s * CAP : (s + 1) * CAP, :] = total.reshape(owners, CAP, vals.shape[2])
        lane_pick = (iota((LANES, rows), 0) == rank + s * CAP).astype(BF16)
        named = (hits_f * (coarse[s : s + 1, :] + 1).astype(F32)).astype(BF16)
        targets = targets + lax.dot_general(
            named, lane_pick, (((1,), (1,)), ((), ())), preferred_element_type=F32
        )
    for o in range(owners):
        tgt[o] = targets[o : o + 1, :]
    cy = e.shape[0]
    lane = iota((cy, LANES), 1)

    def put(base, tile, at, width):
        moved = pltpu.roll(tile, at % LANES, 1) if at % LANES else tile
        return jnp.where((lane >= at) & (lane < at + width), moved, base)

    first = e[...]
    for k, ref in ((1, u), (2, v)):
        first = put(first, ref[...], k * STATE_HI, STATE_HI)
    hi[:, :LANES] = first
    second = depth[0][...]
    last = jnp.zeros((cy, LANES), F32)
    for k in range(STEPS + 1):
        if k:
            second = put(second, wet[0][k - 1].astype(F32), starts(AUX_HI)[k], AUX_HI[k])
        tile = wet[1][k - 1].astype(F32) if k else depth[1][...]
        at = starts(AUX_LO)[k]
        moved = pltpu.roll(tile, (at + AUX_LO[k]) % LANES, 1)
        last = jnp.where((lane >= at) & (lane < at + AUX_LO[k]), moved, last)
    hi[:, LANES:] = second
    lo[...] = last
    mine = eowner[...] == lax.axis_index("nx")
    edge[...] = jnp.where(mine, epanel[:, 0, :], 0.0)


def comm_kernel(ny, nx, n_halo, send, tgt, e, u, v, depth, wet, hi_p, lo_p, edge_p,
                srs, srd, srw0, srw1, srw2, srw3, nrd, nrw, hi, lo, fc, edges,
                got, got_t, own, a_ssem, a_rsem, h_ssem, h_rsem, f_ssem, f_rsem,
                e_ssem, e_rsem, l_sem):
    y, x = lax.axis_index("ny"), lax.axis_index("nx")
    owners = ny * nx
    me = y * nx + x
    cy = e.shape[0]

    def remote(src, dst, ss, rs, ty, tx):
        return pltpu.make_async_remote_copy(
            src_ref=src, dst_ref=dst, send_sem=ss, recv_sem=rs,
            device_id=(ty, tx), device_id_type=MESH)

    def to_owner(k):
        t = lax.rem(me + k, owners)
        ty, tx = t // nx, lax.rem(t, nx)
        return (remote(send.at[t], got.at[me], a_ssem.at[0], a_rsem.at[0], ty, tx),
                remote(tgt.at[t], got_t.at[me], a_ssem.at[1], a_rsem.at[1], ty, tx))

    def start_owner(k, carry):
        for copy in to_owner(k):
            copy.start()
        return carry

    lax.fori_loop(1, owners, start_owner, 0)
    self_v = pltpu.make_async_copy(send.at[me], got.at[me], a_rsem.at[0])
    self_t = pltpu.make_async_copy(tgt.at[me], got_t.at[me], a_rsem.at[1])
    self_v.start()
    self_t.start()

    def sends_to(dy, dx):
        terms = []
        if dy:
            terms.append(y > 0 if dy < 0 else y < ny - 1)
        if dx:
            terms.append(x > 0 if dx < 0 else x < nx - 1)
        return functools.reduce(jnp.logical_and, terms)

    wet_rows = [srw0, srw1, srw2, srw3]
    plan = [(-1, 0, ref.at[pl.ds(0, STATE_HI)], srs.at[k]) for k, ref in enumerate((e, u, v))]
    plan.append((-1, 0, depth.at[pl.ds(0, srd.shape[0])], srd))
    for s in range(STEPS):
        plan.append((-1, 0, wet.at[s, pl.ds(0, wet_rows[s].shape[0])], wet_rows[s]))
    end = pl.ds(cy - PAD, PAD)
    plan.append((1, 0, depth.at[end], nrd))
    plan.append((1, 0, wet.at[:, end], nrw))
    low_rows = lo.shape[0] - PAD - cy
    plan.append((0, -1, hi_p, hi.at[pl.ds(PAD, cy)]))
    plan.append((0, 1, lo_p, lo.at[pl.ds(PAD, cy)]))
    plan.append((-1, -1, hi_p.at[pl.ds(0, STATE_HI)], hi.at[pl.ds(PAD + cy, STATE_HI)]))
    plan.append((1, -1, hi_p.at[end], hi.at[pl.ds(0, PAD)]))
    plan.append((-1, 1, lo_p.at[pl.ds(0, low_rows)], lo.at[pl.ds(PAD + cy, low_rows)]))
    plan.append((1, 1, lo_p.at[end], lo.at[pl.ds(0, PAD)]))
    assert len(plan) == n_halo
    halos = []
    for k, (dy, dx, src, dst) in enumerate(plan):
        copy = remote(src, dst, h_ssem.at[k], h_rsem.at[k], y + dy, x + dx)
        halos.append((copy, dy, dx))
        pl.when(sends_to(dy, dx))(copy.start)

    for dy in (-1, 0, 1):
        copy = remote(edge_p, edges.at[1 - dy, x], e_ssem.at[1 - dy], e_rsem.at[1 - dy],
                      y + dy, x * 0)
        there = (x > 0) if dy == 0 else sends_to(dy, 0)
        pl.when(there)(copy.start)
    self_e = pltpu.make_async_copy(edge_p, edges.at[1, 0], e_rsem.at[1])
    pl.when(x == 0)(self_e.start)

    pltpu.make_async_copy(got, got, a_rsem.at[0]).wait()
    pltpu.make_async_copy(got_t, got_t, a_rsem.at[1]).wait()
    n_coarse, n_cols = own.shape[1], own.shape[2]
    places = owners * CAP
    named = got_t[:, 0, :].astype(BF16)
    place_owner = iota((owners, places), 1) // CAP
    own_place = place_owner == iota((owners, places), 0)
    slot = iota((LANES, places), 1) - iota((LANES, places), 1) // CAP * CAP
    for s in range(STEPS):
        spread = (iota((LANES, places), 0) == slot + s * CAP).astype(BF16)
        wide = jnp.dot(named, spread, preferred_element_type=F32)
        target = jnp.sum(jnp.where(own_place, wide, 0.0), axis=0, keepdims=True)
        pick = (iota((n_coarse, places), 0).astype(F32) == target - 1.0).astype(BF16)
        values = got[:, s * CAP : (s + 1) * CAP, :].reshape(places, n_cols)
        total = jnp.zeros((n_coarse, n_cols), F32)
        for piece in pieces(values):
            total = total + jnp.dot(pick, piece, preferred_element_type=F32)
        own[s] = total
    half = n_coarse // 2
    self_f = pltpu.make_async_copy(own, fc.at[4], l_sem.at[0])
    self_f.start()
    coarse = []
    for dy in (-1, 0, 1):
        for dx in (-1, 0, 1):
            if dy == 0 and dx == 0:
                continue
            k = (1 - dy) * 3 + (1 - dx)
            part = {-1: pl.ds(0, half), 0: pl.ds(0, n_coarse), 1: pl.ds(half, half)}[dy]
            copy = remote(own.at[:, part], fc.at[k, :, part], f_ssem.at[k], f_rsem.at[k],
                          y + dy, x + dx)
            coarse.append((copy, dy, dx))
            pl.when(sends_to(dy, dx))(copy.start)
    for copy, dy, dx in halos + coarse:
        pl.when(sends_to(-dy, -dx))(copy.wait_recv)
    for dy in (-1, 0, 1):
        whole = edges.at[1 - dy]
        here = (x == 0) if dy == 0 else jnp.logical_and(x == 0, sends_to(-dy, 0))
        pl.when(here)(pltpu.make_async_copy(whole, whole, e_rsem.at[1 - dy]).wait)
    for copy, dy, dx in halos + coarse:
        pl.when(sends_to(dy, dx))(copy.wait_send)
    for dy in (-1, 0, 1):
        copy = remote(edge_p, edges.at[1 - dy, x], e_ssem.at[1 - dy], e_rsem.at[1 - dy],
                      y + dy, x * 0)
        there = (x > 0) if dy == 0 else sends_to(dy, 0)
        pl.when(there)(copy.wait_send)
    self_f.wait()

    def end_owner(k, carry):
        for copy in to_owner(k):
            copy.wait_send()
        return carry

    lax.fori_loop(1, owners, end_owner, 0)


def step_kernel(ny, nx, shifts, e, u, v, depth, wet, srs, srd, srw0, srw1, srw2, srw3,
                nrd, nrw, hi, lo, fc, edges, out_e, out_u, out_v,
                ext, ext_d, ext_w, hi_v, lo_v, edge_v, fc_v, work, cur, force, sems):
    y, x = lax.axis_index("ny"), lax.axis_index("nx")
    cy, cx = e.shape
    width = ext.shape[2]
    win = cur.shape[1]
    halo = srs.shape[1]
    own_cols = pl.ds(0, cx)
    groups = [[], [], [], [], [], []]
    groups[0] += [(hi, hi_v), (lo, lo_v), (fc, fc_v), (edges, edge_v)]
    for k, ref in enumerate((e, u, v)):
        groups[1].append((ref, ext.at[k, pl.ds(0, cy), own_cols]))
        groups[1].append((srs.at[k], ext.at[k, pl.ds(cy, halo), own_cols]))
    groups[1].append((nrd, ext_d.at[pl.ds(0, PAD), own_cols]))
    groups[1].append((depth, ext_d.at[pl.ds(PAD, cy), own_cols]))
    groups[1].append((srd, ext_d.at[pl.ds(PAD + cy, srd.shape[0]), own_cols]))
    for s, rows in enumerate((srw0, srw1, srw2, srw3)):
        groups[2 + s].append((nrw.at[s], ext_w.at[s, pl.ds(0, PAD), own_cols]))
        groups[2 + s].append((wet.at[s], ext_w.at[s, pl.ds(PAD, cy), own_cols]))
        groups[2 + s].append((rows, ext_w.at[s, pl.ds(PAD + cy, rows.shape[0]), own_cols]))
    copies = []
    count = 0
    for group in groups:
        made = []
        for src, dst in group:
            made.append(pltpu.make_async_copy(src, dst, sems.at[count]))
            made[-1].start()
            count += 1
        copies.append(made)

    def finish(group):
        for copy in copies[group]:
            copy.wait()

    sum_r = [sum([shifts[t, 0] for t in range(s, STEPS)], jnp.int32(0)) for s in range(STEPS + 1)]
    sum_c = [sum([shifts[t, 1] for t in range(s, STEPS)], jnp.int32(0)) for s in range(STEPS + 1)]

    finish(0)
    n_coarse, n_cols = fc.shape[2], fc.shape[3]
    has_y = {-1: y > 0, 0: y >= 0, 1: y < ny - 1}
    has_x = {-1: x > 0, 0: x >= 0, 1: x < nx - 1}
    half = n_coarse // 2

    def weights(fine, which, at, fine_count, coarse_count):
        inner = fine - which * fine_count
        spot = jnp.clip(2 * inner + 1 - RATIO, 0, 2 * RATIO * (coarse_count - 1))
        weight = jnp.maximum(2 * RATIO - jnp.abs(spot - 2 * RATIO * at), 0)
        inside = (inner >= 0) & (inner < fine_count)
        return jnp.where(inside, weight, 0).astype(F32).astype(BF16)

    lane_e = iota((n_coarse, n_cols), 1)
    row_e = iota((n_coarse, n_cols), 0)

    def forcing(s):
        q = iota((win, 3 * n_coarse), 1)
        which = (q >= n_coarse).astype(I32) + (q >= 2 * n_coarse).astype(I32) - 1
        fine = iota((win, 3 * n_coarse), 0) - PAD + sum_r[s + 1]
        row_w = weights(fine, which, q - (which + 1) * n_coarse, cy, n_coarse)
        bands = []
        for dy in (-1, 0, 1):
            sides = {}
            for dx in (-1, 0, 1):
                ok = has_y[dy] & has_x[dx]
                block = fc_v[(dy + 1) * 3 + dx + 1, s]
                if dy:
                    ok = ok & ((row_e >= half) if dy < 0 else (row_e < half))
                sides[dx] = jnp.where(ok, block, 0.0)
            beside = jnp.where(lane_e < n_cols // 2, sides[1], sides[-1])
            bands.append(jnp.concatenate([sides[0], beside], axis=1))
        coarse = jnp.concatenate(bands, axis=0)
        section = jnp.zeros((win, 2 * n_cols), F32)
        for piece in pieces(coarse):
            section = section + jnp.dot(row_w, piece, preferred_element_type=F32)
        q = iota((2 * n_cols, width), 0)
        at = q - jnp.where(q >= n_cols, n_cols, 0)
        which = jnp.where(q < n_cols, 0, jnp.where(at < n_cols // 2, 1, -1))
        lane = iota((2 * n_cols, width), 1)
        fine = lane - jnp.where(lane >= width - PAD, width, 0) + sum_c[s + 1]
        col_w = weights(fine, which, at, cx, n_cols)
        total = jnp.zeros((win, width), F32)
        for piece in pieces(section):
            total = total + jnp.dot(piece, col_w, preferred_element_type=F32)
        force[...] = total * (1.0 / (4.0 * RATIO * RATIO))

    rows_here = hi_v.shape[0]
    lane_t = iota((rows_here, LANES), 1)

    def moved(tile, by):
        by = by % LANES
        return pltpu.roll(tile, by, 1) if by else tile

    for k in range(3):
        ext[k, pl.ds(0, cy + halo), cx : cx + LANES] = moved(
            hi_v[pl.ds(PAD, cy + halo), :LANES], -k * STATE_HI)
    high = hi_v[:, LANES:]
    for k in range(STEPS + 1):
        high_k = moved(high, -starts(AUX_HI)[k])
        low_k = moved(lo_v[...], -(starts(AUX_LO)[k] + AUX_LO[k]))
        tile = jnp.where(lane_t < LANES // 2, high_k, low_k)
        if k == 0:
            ext_d[pl.ds(0, rows_here), cx : cx + LANES] = tile
        else:
            ext_w[k - 1, pl.ds(0, rows_here), cx : cx + LANES] = tile.astype(I32)

    def rows_at(load, start):
        base = pl.multiple_of(start // PAD * PAD, PAD)
        both = load(pl.ds(base, 2 * PAD))
        return pltpu.roll(both, lax.rem(2 * PAD - (start - base), 2 * PAD), 0)[:PAD]

    lane = iota((PAD, width), 1)
    row = iota((PAD, width), 0)
    row_1 = iota((PAD, 1), 0)
    col_local = lane - jnp.where(lane >= width - PAD, width, 0)
    edge_sum = jnp.sum(edge_v[...], axis=1)

    for s in range(STEPS):
        forcing(s)
        if s == 0:
            finish(1)
        finish(2 + s)
        off_r, off_c = sum_r[s + 1], sum_c[s + 1]
        gcol = col_local + (x * cx + off_c)
        col_in = (gcol >= 0) & (gcol < nx * cx)
        col_ok = col_in & (gcol + shifts[s, 1] < nx * cx)
        ghost_col = gcol == -1
        back = lax.rem(width - off_c, width)
        back_0 = lax.rem(width - sum_c[0], width)
        edge_rows = [edge_sum[d, s : s + 1, :] for d in range(3)]

        def fill(t, carry):
            a = pl.multiple_of(t * PAD, PAD)
            local = row + (a - PAD) + off_r
            grow = local + y * cy
            row_in = (grow >= 0) & (grow < ny * cy)
            inside = row_in & col_in
            valid = row_in & col_ok & (grow + shifts[s, 0] < ny * cy)
            fields = []
            for k in range(3):
                if s == 0:
                    piece = rows_at(lambda at: ext[k, at, :], a - PAD + sum_r[0])
                    piece = pltpu.roll(piece, back_0, 1)
                else:
                    piece = cur[k, pl.ds(a, PAD), :]
                fields.append(jnp.where(valid, piece, 0.0))
            surface = jnp.where(inside, fields[0] + force[pl.ds(a, PAD), :], 0.0)
            mask = rows_at(lambda at: ext_w[s, at, :], a + off_r)
            mask = jnp.where(inside, pltpu.roll(mask, back, 1).astype(F32), 0.0)
            bed = rows_at(lambda at: ext_d[at, :], a + off_r)
            bed = jnp.where(inside, pltpu.roll(bed, back, 1), 0.0)
            spot = row_1 + (a - PAD) + off_r
            value = jnp.zeros((PAD, 1), F32)
            for d in range(3):
                at = iota((PAD, cy), 1) + (d - 1) * cy
                value = value + jnp.sum(
                    jnp.where(at == spot, edge_rows[d], 0.0), axis=1, keepdims=True)
            ghost = ghost_col & row_in
            surface = jnp.where(ghost, value, surface)
            mask = jnp.where(ghost, 1.0, mask)
            for k, field in enumerate((surface, fields[1], fields[2], mask, bed)):
                work[k, pl.ds(a + PAD, PAD), :] = field
            return carry

        lax.fori_loop(0, win // PAD, fill, 0)

        def advance(t, carry):
            a = pl.multiple_of(t * PAD, PAD)
            around = [work[k, pl.ds(a, 3 * PAD), :] for k in range(5)]
            here = [f[PAD : 2 * PAD] for f in around]

            def faces(low, up, normal, cross):
                e_l, m_l, b_l = low[0], low[3], low[4]
                e_h, m_h, b_h = up[0], up[3], up[4]
                opened = m_l * m_h
                thin = 0.25 * opened
                rise = e_h - e_l
                level = e_h + e_l
                n_l, n_h = low[normal], up[normal]
                mass = thin * (2.0 * (n_l + n_h) - rise)
                push = thin * ((b_l + b_h) * level - (n_h - n_l))
                shear = thin * (low[cross] - up[cross])
                return mass, push, shear

            east = [pltpu.roll(f, width - 1, 1) for f in here]
            flux = faces(here, east, 1, 2)
            total = [f - pltpu.roll(f, 1, 1) for f in flux]
            upper = [f[PAD + 1 : 2 * PAD + 1] for f in around]
            lower = [f[PAD - 1 : 2 * PAD - 1] for f in around]
            f_n = faces(here, upper, 2, 1)
            f_s = faces(lower, here, 2, 1)
            d_mass, d_push, d_shear = [p - q for p, q in zip(f_n, f_s)]
            new = (
                here[0] - 0.25 * (total[0] + d_mass),
                here[3] * (here[1] - 0.25 * (total[1] + d_shear)),
                here[3] * (here[2] - 0.25 * (total[2] + d_push)),
            )
            for k in range(3):
                if s == STEPS - 1:
                    (out_e, out_u, out_v)[k][pl.ds(pl.multiple_of(a - PAD, PAD), PAD), :] = new[k][:, :cx]
                else:
                    cur[k, pl.ds(a, PAD), :] = new[k]
            return carry

        if s == STEPS - 1:
            lax.fori_loop(1, 1 + cy // PAD, advance, 0)
        else:
            lax.fori_loop(0, win // PAD, advance, 0)


def local(elevation, flux_x, flux_y, depth, wet_mask, shifts, parent_vals, row_dest, row_coarse,
          edge_owner, edge_panels):
    cy, cx = elevation.shape
    ny, nx = lax.axis_size("ny"), lax.axis_size("nx")
    owners = ny * nx
    n_cols = parent_vals.shape[2]
    n_coarse = cy // RATIO
    sds = jax.ShapeDtypeStruct
    any_ = pl.BlockSpec(memory_space=pl.ANY)
    vm = pl.BlockSpec(memory_space=pltpu.VMEM)
    sm = pl.BlockSpec(memory_space=pltpu.SMEM)

    def whole(ndim, shape):
        return pl.BlockSpec(shape, lambda i: (0,) * ndim)

    last = cx // LANES - 1
    send, tgt, hi_p, lo_p, edge_p = pl.pallas_call(
        functools.partial(prep_kernel, owners),
        out_shape=(
            sds((owners, STEPS * CAP, n_cols), F32),
            sds((owners, 1, LANES), F32),
            sds((cy, 2 * LANES), F32),
            sds((cy, LANES), F32),
            sds((STEPS, cy), F32),
        ),
        grid=(1,),
        in_specs=[
            whole(2, row_dest.shape), whole(2, row_coarse.shape), whole(3, parent_vals.shape),
            pl.BlockSpec((cy, LANES), lambda i: (0, 0)),
            pl.BlockSpec((cy, LANES), lambda i: (0, 0)),
            pl.BlockSpec((cy, LANES), lambda i: (0, 0)),
            pl.BlockSpec((cy, LANES), lambda i: (0, 0)),
            pl.BlockSpec((cy, LANES), lambda i: (0, last)),
            pl.BlockSpec((STEPS, cy, LANES), lambda i: (0, 0, 0)),
            pl.BlockSpec((STEPS, cy, LANES), lambda i: (0, 0, last)),
            whole(2, edge_owner.shape), whole(3, edge_panels.shape),
        ],
        name="prep",
    )(row_dest, row_coarse, parent_vals, elevation, flux_x, flux_y, depth, depth, wet_mask,
      wet_mask, edge_owner, edge_panels)

    n_halo = 16
    wet_hi = [round_up(w, PAD) for w in WET_HI]
    dma = pltpu.SemaphoreType.DMA
    halos = pl.pallas_call(
        functools.partial(comm_kernel, ny, nx, n_halo),
        out_shape=(
            sds((3, STATE_HI, cx), F32), sds((wet_hi[0], cx), F32),
            *[sds((w, cx), I32) for w in wet_hi],
            sds((PAD, cx), F32), sds((STEPS, PAD, cx), I32),
            sds((PAD + cy + STATE_HI, 2 * LANES), F32),
            sds((PAD + cy + STATE_HI, LANES), F32),
            sds((9, STEPS, n_coarse, n_cols), F32),
            sds((3, nx, STEPS, cy), F32),
        ),
        in_specs=[any_] * 10,
        out_specs=(any_,) * 12,
        scratch_shapes=[
            pltpu.VMEM((owners, STEPS * CAP, n_cols), F32),
            pltpu.VMEM((owners, 1, LANES), F32),
            pltpu.VMEM((STEPS, n_coarse, n_cols), F32),
            dma((2,)), dma((2,)), dma((n_halo,)), dma((n_halo,)), dma((9,)), dma((9,)),
            dma((3,)), dma((3,)), dma((1,)),
        ],
        compiler_params=pltpu.CompilerParams(has_side_effects=True),
        name="exchange",
    )(send, tgt, elevation, flux_x, flux_y, depth, wet_mask, hi_p, lo_p, edge_p)

    width = cx + LANES
    rows = PAD + cy + STATE_HI
    ext_rows = rows + PAD
    win = cy + 2 * PAD
    return pl.pallas_call(
        functools.partial(step_kernel, ny, nx),
        out_shape=(sds((cy, cx), F32),) * 3,
        in_specs=[sm] + [any_] * 17,
        out_specs=(vm,) * 3,
        scratch_shapes=[
            pltpu.VMEM((3, ext_rows, width), F32),
            pltpu.VMEM((ext_rows, width), F32),
            pltpu.VMEM((STEPS, ext_rows, width), I32),
            pltpu.VMEM((rows, 2 * LANES), F32),
            pltpu.VMEM((rows, LANES), F32),
            pltpu.VMEM((3, nx, STEPS, cy), F32),
            pltpu.VMEM((9, STEPS, n_coarse, n_cols), F32),
            pltpu.VMEM((5, win + 2 * PAD, width), F32),
            pltpu.VMEM((3, win, width), F32),
            pltpu.VMEM((win, width), F32),
            dma((32,)),
        ],
        compiler_params=pltpu.CompilerParams(vmem_limit_bytes=56 * 1024 * 1024),
        name="steps",
    )(shifts, elevation, flux_x, flux_y, depth, wet_mask, *halos)


def solution(mesh):
    in_specs = (
        P("ny", "nx"),
        P("ny", "nx"),
        P("ny", "nx"),
        P("ny", "nx"),
        P(None, "ny", "nx"),
        P(),
        P(None, ("ny", "nx"), None),
        P(None, ("ny", "nx")),
        P(None, ("ny", "nx")),
        P(None, "ny"),
        P(None, "nx", "ny"),
    )
    out_specs = (P("ny", "nx"), P("ny", "nx"), P("ny", "nx"))
    return jax.shard_map(local, mesh=mesh, in_specs=in_specs, out_specs=out_specs, check_vma=False)
```

```python
import functools

import jax
import jax.numpy as jnp
from jax import lax
from jax.experimental import pallas as pl
from jax.experimental.pallas import tpu as pltpu
from jax.sharding import PartitionSpec as P

RATIO = 9
STEPS = 4
SH = 9
CAP = 8
PAD = 8
LANES = 128
MESH = pl.DeviceIdType.MESH
F32 = jnp.float32
BF16 = jnp.bfloat16
I32 = jnp.int32

STATE_HI = STEPS * (SH + 1)
WET_HI = [SH * (STEPS - 1 - s) + STEPS - s for s in range(STEPS)]
WET_LO = [STEPS - s for s in range(STEPS)]
AUX_HI = [WET_HI[0]] + WET_HI
AUX_LO = [WET_LO[0]] + WET_LO


def starts(widths):
    return [sum(widths[:k]) for k in range(len(widths))]


def round_up(value, unit):
    return -(-value // unit) * unit


def pieces(value):
    high = value.astype(BF16)
    rest = value - high.astype(F32)
    mid = rest.astype(BF16)
    low = (rest - mid.astype(F32)).astype(BF16)
    return high, mid, low


def iota(shape, dim):
    return lax.broadcasted_iota(I32, shape, dim)


def prep_kernel(owners, dest, coarse, vals, e, u, v, d_0, d_1, w_0, w_1, eowner, epanel,
                send, tgt, hi, lo, edge):
    depth, wet = (d_0, d_1), (w_0, w_1)
    rows = dest.shape[1]
    places = owners * CAP
    before = (iota((rows, rows), 0) < iota((rows, rows), 1)).astype(BF16)
    targets = jnp.zeros((owners, LANES), F32)
    for s in range(STEPS):
        d = dest[s : s + 1, :]
        hits = iota((owners, rows), 0) == d
        hits_f = hits.astype(F32)
        earlier = jnp.dot(hits.astype(BF16), before, preferred_element_type=F32)
        rank = jnp.sum(hits_f * earlier, axis=0, keepdims=True).astype(I32)
        place = d * CAP + rank
        pick = (iota((places, rows), 0) == place).astype(BF16)
        total = jnp.zeros((places, vals.shape[2]), F32)
        for piece in pieces(vals[s]):
            total = total + jnp.dot(pick, piece, preferred_element_type=F32)
        send[:, s * CAP : (s + 1) * CAP, :] = total.reshape(owners, CAP, vals.shape[2])
        lane_pick = (iota((LANES, rows), 0) == rank + s * CAP).astype(BF16)
        named = (hits_f * (coarse[s : s + 1, :] + 1).astype(F32)).astype(BF16)
        targets = targets + lax.dot_general(
            named, lane_pick, (((1,), (1,)), ((), ())), preferred_element_type=F32
        )
    for o in range(owners):
        tgt[o] = targets[o : o + 1, :]
    cy = e.shape[0]
    lane = iota((cy, LANES), 1)

    def put(base, tile, at, width):
        moved = pltpu.roll(tile, at % LANES, 1) if at % LANES else tile
        return jnp.where((lane >= at) & (lane < at + width), moved, base)

    first = e[...]
    for k, ref in ((1, u), (2, v)):
        first = put(first, ref[...], k * STATE_HI, STATE_HI)
    hi[:, :LANES] = first
    second = depth[0][...]
    last = jnp.zeros((cy, LANES), F32)
    for k in range(STEPS + 1):
        if k:
            second = put(second, wet[0][k - 1].astype(F32), starts(AUX_HI)[k], AUX_HI[k])
        tile = wet[1][k - 1].astype(F32) if k else depth[1][...]
        at = starts(AUX_LO)[k]
        moved = pltpu.roll(tile, (at + AUX_LO[k]) % LANES, 1)
        last = jnp.where((lane >= at) & (lane < at + AUX_LO[k]), moved, last)
    hi[:, LANES:] = second
    lo[...] = last
    for s in range(STEPS):
        mine = eowner[:, s : s + 1] == lax.axis_index("nx")
        edge[s : s + 1, :] = jnp.where(mine, epanel[s], 0.0)


def comm_kernel(ny, nx, n_halo, send, tgt, e, u, v, depth, wet, hi_p, lo_p, edge_p,
                srs, srd, srw0, srw1, srw2, srw3, nrd, nrw, hi, lo, fc, edges,
                got, got_t, own, a_ssem, a_rsem, h_ssem, h_rsem, f_ssem, f_rsem,
                e_ssem, e_rsem, l_sem):
    y, x = lax.axis_index("ny"), lax.axis_index("nx")
    owners = ny * nx
    me = y * nx + x
    cy = e.shape[0]

    def remote(src, dst, ss, rs, ty, tx):
        return pltpu.make_async_remote_copy(
            src_ref=src, dst_ref=dst, send_sem=ss, recv_sem=rs,
            device_id=(ty, tx), device_id_type=MESH)

    def to_owner(k):
        t = lax.rem(me + k, owners)
        ty, tx = t // nx, lax.rem(t, nx)
        return (remote(send.at[t], got.at[me], a_ssem.at[0], a_rsem.at[0], ty, tx),
                remote(tgt.at[t], got_t.at[me], a_ssem.at[1], a_rsem.at[1], ty, tx))

    def start_owner(k, carry):
        for copy in to_owner(k):
            copy.start()
        return carry

    lax.fori_loop(1, owners, start_owner, 0)
    self_v = pltpu.make_async_copy(send.at[me], got.at[me], a_rsem.at[0])
    self_t = pltpu.make_async_copy(tgt.at[me], got_t.at[me], a_rsem.at[1])
    self_v.start()
    self_t.start()

    def sends_to(dy, dx):
        terms = []
        if dy:
            terms.append(y > 0 if dy < 0 else y < ny - 1)
        if dx:
            terms.append(x > 0 if dx < 0 else x < nx - 1)
        return functools.reduce(jnp.logical_and, terms)

    wet_rows = [srw0, srw1, srw2, srw3]
    plan = [(-1, 0, ref.at[pl.ds(0, STATE_HI)], srs.at[k]) for k, ref in enumerate((e, u, v))]
    plan.append((-1, 0, depth.at[pl.ds(0, srd.shape[0])], srd))
    for s in range(STEPS):
        plan.append((-1, 0, wet.at[s, pl.ds(0, wet_rows[s].shape[0])], wet_rows[s]))
    end = pl.ds(cy - PAD, PAD)
    plan.append((1, 0, depth.at[end], nrd))
    plan.append((1, 0, wet.at[:, end], nrw))
    low_rows = lo.shape[0] - PAD - cy
    plan.append((0, -1, hi_p, hi.at[pl.ds(PAD, cy)]))
    plan.append((0, 1, lo_p, lo.at[pl.ds(PAD, cy)]))
    plan.append((-1, -1, hi_p.at[pl.ds(0, STATE_HI)], hi.at[pl.ds(PAD + cy, STATE_HI)]))
    plan.append((1, -1, hi_p.at[end], hi.at[pl.ds(0, PAD)]))
    plan.append((-1, 1, lo_p.at[pl.ds(0, low_rows)], lo.at[pl.ds(PAD + cy, low_rows)]))
    plan.append((1, 1, lo_p.at[end], lo.at[pl.ds(0, PAD)]))
    assert len(plan) == n_halo
    halos = []
    for k, (dy, dx, src, dst) in enumerate(plan):
        copy = remote(src, dst, h_ssem.at[k], h_rsem.at[k], y + dy, x + dx)
        halos.append((copy, dy, dx))
        pl.when(sends_to(dy, dx))(copy.start)

    for dy in (-1, 0, 1):
        copy = remote(edge_p, edges.at[1 - dy, x], e_ssem.at[1 - dy], e_rsem.at[1 - dy],
                      y + dy, x * 0)
        there = (x > 0) if dy == 0 else sends_to(dy, 0)
        pl.when(there)(copy.start)
    self_e = pltpu.make_async_copy(edge_p, edges.at[1, 0], e_rsem.at[1])
    pl.when(x == 0)(self_e.start)

    pltpu.make_async_copy(got, got, a_rsem.at[0]).wait()
    pltpu.make_async_copy(got_t, got_t, a_rsem.at[1]).wait()
    n_coarse, n_cols = own.shape[1], own.shape[2]
    places = owners * CAP
    named = got_t[:, 0, :].astype(BF16)
    place_owner = iota((owners, places), 1) // CAP
    own_place = place_owner == iota((owners, places), 0)
    slot = iota((LANES, places), 1) - iota((LANES, places), 1) // CAP * CAP
    for s in range(STEPS):
        spread = (iota((LANES, places), 0) == slot + s * CAP).astype(BF16)
        wide = jnp.dot(named, spread, preferred_element_type=F32)
        target = jnp.sum(jnp.where(own_place, wide, 0.0), axis=0, keepdims=True)
        pick = (iota((n_coarse, places), 0).astype(F32) == target - 1.0).astype(BF16)
        values = got[:, s * CAP : (s + 1) * CAP, :].reshape(places, n_cols)
        total = jnp.zeros((n_coarse, n_cols), F32)
        for piece in pieces(values):
            total = total + jnp.dot(pick, piece, preferred_element_type=F32)
        own[s] = total
    half = n_coarse // 2
    self_f = pltpu.make_async_copy(own, fc.at[4], l_sem.at[0])
    self_f.start()
    coarse = []
    for dy in (-1, 0, 1):
        for dx in (-1, 0, 1):
            if dy == 0 and dx == 0:
                continue
            k = (1 - dy) * 3 + (1 - dx)
            part = {-1: pl.ds(0, half), 0: pl.ds(0, n_coarse), 1: pl.ds(half, half)}[dy]
            copy = remote(own.at[:, part], fc.at[k, :, part], f_ssem.at[k], f_rsem.at[k],
                          y + dy, x + dx)
            coarse.append((copy, dy, dx))
            pl.when(sends_to(dy, dx))(copy.start)
    for copy, dy, dx in halos + coarse:
        pl.when(sends_to(-dy, -dx))(copy.wait_recv)
    for dy in (-1, 0, 1):
        whole = edges.at[1 - dy]
        here = (x == 0) if dy == 0 else jnp.logical_and(x == 0, sends_to(-dy, 0))
        pl.when(here)(pltpu.make_async_copy(whole, whole, e_rsem.at[1 - dy]).wait)
    for copy, dy, dx in halos + coarse:
        pl.when(sends_to(dy, dx))(copy.wait_send)
    for dy in (-1, 0, 1):
        copy = remote(edge_p, edges.at[1 - dy, x], e_ssem.at[1 - dy], e_rsem.at[1 - dy],
                      y + dy, x * 0)
        there = (x > 0) if dy == 0 else sends_to(dy, 0)
        pl.when(there)(copy.wait_send)
    self_f.wait()

    def end_owner(k, carry):
        for copy in to_owner(k):
            copy.wait_send()
        return carry

    lax.fori_loop(1, owners, end_owner, 0)


def step_kernel(ny, nx, shifts, e, u, v, depth, wet, srs, srd, srw0, srw1, srw2, srw3,
                nrd, nrw, hi, lo, fc, edges, out_e, out_u, out_v,
                ext, ext_d, ext_w, hi_v, lo_v, edge_v, fc_v, work, cur, force, col_w, prev, sems):
    y, x = lax.axis_index("ny"), lax.axis_index("nx")
    cy, cx = e.shape
    width = ext.shape[2]
    win = cur.shape[1]
    halo = srs.shape[1]
    own_cols = pl.ds(0, cx)
    groups = [[], [], [], [], [], []]
    groups[0] += [(hi, hi_v), (lo, lo_v), (fc, fc_v), (edges, edge_v)]
    for k, ref in enumerate((e, u, v)):
        groups[1].append((ref, ext.at[k, pl.ds(0, cy), own_cols]))
        groups[1].append((srs.at[k], ext.at[k, pl.ds(cy, halo), own_cols]))
    groups[1].append((nrd, ext_d.at[pl.ds(0, PAD), own_cols]))
    groups[1].append((depth, ext_d.at[pl.ds(PAD, cy), own_cols]))
    groups[1].append((srd, ext_d.at[pl.ds(PAD + cy, srd.shape[0]), own_cols]))
    for s, rows in enumerate((srw0, srw1, srw2, srw3)):
        groups[2 + s].append((nrw.at[s], ext_w.at[s, pl.ds(0, PAD), own_cols]))
        groups[2 + s].append((wet.at[s], ext_w.at[s, pl.ds(PAD, cy), own_cols]))
        groups[2 + s].append((rows, ext_w.at[s, pl.ds(PAD + cy, rows.shape[0]), own_cols]))
    copies = []
    count = 0
    for group in groups:
        made = []
        for src, dst in group:
            made.append(pltpu.make_async_copy(src, dst, sems.at[count]))
            made[-1].start()
            count += 1
        copies.append(made)

    def finish(group):
        for copy in copies[group]:
            copy.wait()

    sum_r = [sum([shifts[0, t] for t in range(s, STEPS)], jnp.int32(0)) for s in range(STEPS + 1)]
    sum_c = [sum([shifts[1, t] for t in range(s, STEPS)], jnp.int32(0)) for s in range(STEPS + 1)]

    n_coarse, n_cols = fc.shape[2], fc.shape[3]
    has_y = {-1: y > 0, 0: y >= 0, 1: y < ny - 1}
    has_x = {-1: x > 0, 0: x >= 0, 1: x < nx - 1}
    half = n_coarse // 2

    def weights(fine, which, at, fine_count, coarse_count):
        inner = fine - which * fine_count
        spot = jnp.clip(2 * inner + 1 - RATIO, 0, 2 * RATIO * (coarse_count - 1))
        weight = jnp.maximum(2 * RATIO - jnp.abs(spot - 2 * RATIO * at), 0)
        inside = (inner >= 0) & (inner < fine_count)
        return jnp.where(inside, weight, 0).astype(F32).astype(BF16)

    tiles = width // LANES
    lane = iota((PAD, LANES), 1)
    row = iota((PAD, LANES), 0)

    q = iota((2 * n_cols, LANES), 0)
    at_q = q - jnp.where(q >= n_cols, n_cols, 0)
    which_q = jnp.where(q < n_cols, 0, jnp.where(at_q < n_cols // 2, 1, -1))
    lane_q = iota((2 * n_cols, LANES), 1)
    for k in range(tiles):
        fine = lane_q + k * LANES
        fine = fine - jnp.where(fine >= width - PAD, width, 0)
        col_w[:, k * LANES : (k + 1) * LANES] = weights(fine, which_q, at_q, cx, n_cols)
    finish(0)
    lane_e = iota((n_coarse, n_cols), 1)
    row_e = iota((n_coarse, n_cols), 0)

    def forcing(s):
        q = iota((win, 3 * n_coarse), 1)
        which = (q >= n_coarse).astype(I32) + (q >= 2 * n_coarse).astype(I32) - 1
        fine = iota((win, 3 * n_coarse), 0) - PAD + sum_r[s + 1]
        row_w = weights(fine, which, q - (which + 1) * n_coarse, cy, n_coarse)
        bands = []
        for dy in (-1, 0, 1):
            sides = {}
            for dx in (-1, 0, 1):
                ok = has_y[dy] & has_x[dx]
                block = fc_v[(dy + 1) * 3 + dx + 1, s]
                if dy:
                    ok = ok & ((row_e >= half) if dy < 0 else (row_e < half))
                sides[dx] = jnp.where(ok, block, 0.0)
            beside = jnp.where(lane_e < n_cols // 2, sides[1], sides[-1])
            bands.append(jnp.concatenate([sides[0], beside], axis=1))
        coarse = jnp.concatenate(bands, axis=0)
        section = jnp.zeros((win, 2 * n_cols), F32)
        for piece in pieces(coarse):
            section = section + jnp.dot(row_w, piece, preferred_element_type=F32)
        section = section * (1.0 / (4.0 * RATIO * RATIO))
        total = jnp.zeros((win, width), F32)
        for piece in pieces(section):
            total = total + jnp.dot(piece, col_w[...], preferred_element_type=F32)
        force[...] = total

    rows_here = hi_v.shape[0]
    lane_t = iota((rows_here, LANES), 1)

    def moved(tile, by):
        by = by % LANES
        return pltpu.roll(tile, by, 1) if by else tile

    for k in range(3):
        ext[k, pl.ds(0, cy + halo), cx : cx + LANES] = moved(
            hi_v[pl.ds(PAD, cy + halo), :LANES], -k * STATE_HI)
    high = hi_v[:, LANES:]
    for k in range(STEPS + 1):
        high_k = moved(high, -starts(AUX_HI)[k])
        low_k = moved(lo_v[...], -(starts(AUX_LO)[k] + AUX_LO[k]))
        tile = jnp.where(lane_t < LANES // 2, high_k, low_k)
        if k == 0:
            ext_d[pl.ds(0, rows_here), cx : cx + LANES] = tile
        else:
            ext_w[k - 1, pl.ds(0, rows_here), cx : cx + LANES] = tile.astype(I32)

    edge_sum = jnp.sum(edge_v[...], axis=1)

    def across(pieces_, by):
        turned = [pltpu.roll(f, lax.rem(LANES - by, LANES), 1) for f in pieces_]
        keep = lane < LANES - by
        return [jnp.where(keep, turned[k], turned[(k + 1) % tiles]) for k in range(tiles)]

    def window(load, start, by):
        base = pl.multiple_of(start // PAD * PAD, PAD)
        off = start - base
        turn = lax.rem(PAD - off, PAD)
        upper = row >= off
        out = []
        for k in range(tiles):
            cols = pl.ds(k * LANES, LANES)
            both = jnp.where(upper, load(pl.ds(base, PAD), cols),
                             load(pl.ds(pl.multiple_of(base + PAD, PAD), PAD), cols))
            out.append(pltpu.roll(both, turn, 0))
        return across(out, by)

    def faces(low, up, normal, cross):
        opened = low[3] * up[3]
        thin = 0.25 * opened
        n_l, n_h = low[normal], up[normal]
        mass = thin * (2.0 * (n_l + n_h) - (up[0] - low[0]))
        push = thin * ((low[4] + up[4]) * (up[0] + low[0]) - (n_h - n_l))
        shear = thin * (low[cross] - up[cross])
        return mass, push, shear

    for s in range(STEPS):
        forcing(s)
        if s == 0:
            finish(1)
        finish(2 + s)
        off_r, off_c = sum_r[s + 1], sum_c[s + 1]
        edge_rows = [edge_sum[d, s : s + 1, :] for d in range(3)]

        def fill(t, carry):
            a = pl.multiple_of(t * PAD, PAD)
            here_rows = pl.ds(a, PAD)
            grow = row + (a - PAD) + off_r + y * cy
            row_in = (grow >= 0) & (grow < ny * cy)
            row_ok = row_in & (grow + shifts[0, s] < ny * cy)
            if s == 0:
                fields = [
                    window(lambda r, c: ext[k, r, c], a - PAD + sum_r[0], sum_c[0])
                    for k in range(3)
                ]
            else:
                fields = [
                    [cur[k, here_rows, m * LANES : (m + 1) * LANES] for m in range(tiles)]
                    for k in range(3)
                ]
            wets = window(lambda r, c: ext_w[s, r, c], a + off_r, off_c)
            beds = window(lambda r, c: ext_d[r, c], a + off_r, off_c)
            added = across(
                [force[here_rows, m * LANES : (m + 1) * LANES] for m in range(tiles)], off_c)
            for m in range(tiles):
                valid, inside = row_ok, row_in
                local_col = lane + m * LANES
                if m == tiles - 1:
                    local_col = local_col - jnp.where(local_col >= width - PAD, width, 0)
                gcol = local_col + (x * cx + off_c)
                if (m + 1) * LANES > cx - STEPS * SH:
                    inside = inside & (gcol >= 0) & (gcol < nx * cx)
                    valid = valid & (gcol >= 0) & (gcol + shifts[1, s] < nx * cx)
                e_m = jnp.where(valid, fields[0][m], 0.0) + added[m]
                e_m = jnp.where(inside, e_m, 0.0)
                u_m = jnp.where(valid, fields[1][m], 0.0)
                v_m = jnp.where(valid, fields[2][m], 0.0)
                w_m = jnp.where(inside, wets[m].astype(F32), 0.0)
                b_m = jnp.where(inside, beds[m], 0.0)
                if m == tiles - 1:
                    spot = iota((PAD, cy), 0) + (a - PAD) + off_r
                    at = iota((PAD, cy), 1)
                    value = jnp.zeros((PAD, cy), F32)
                    for d in range(3):
                        value = value + jnp.where(at + (d - 1) * cy == spot, edge_rows[d], 0.0)
                    value = jnp.sum(value, axis=1, keepdims=True)
                    ghost = (gcol == -1) & row_in
                    e_m = jnp.where(ghost, value, e_m)
                    w_m = jnp.where(ghost, 1.0, w_m)
                for k, field in enumerate((e_m, u_m, v_m, w_m, b_m)):
                    work[k, here_rows, m * LANES : (m + 1) * LANES] = field
            return carry

        lax.fori_loop(0, win // PAD, fill, 0)
        last_step = s == STEPS - 1

        def advance(t, keep_result):
            a = pl.multiple_of(t * PAD, PAD)
            rows_a = pl.ds(a, PAD)
            rows_b = pl.ds(pl.multiple_of(a + PAD, PAD), PAD)

            def at(k, rows_, m):
                return work[k, rows_, m * LANES : (m + 1) * LANES]

            def turned_west(m):
                return [pltpu.roll(at(k, rows_a, m), LANES - 1, 1) for k in range(5)]

            def x_faces(here, own, nxt):
                east = [jnp.where(lane < LANES - 1, p, q) for p, q in zip(own, nxt)]
                return faces(here, east, 1, 2)

            n_out = tiles - 1 if last_step else tiles
            first = turned_west(0)
            tail = [at(k, rows_a, tiles - 1) for k in range(5)]
            flux_tail = x_faces(tail, turned_west(tiles - 1), first)
            before = [pltpu.roll(f, 1, 1) for f in flux_tail]
            own = first
            for m in range(n_out):
                here = [at(k, rows_a, m) for k in range(5)]
                if m == tiles - 1:
                    flux = flux_tail
                else:
                    nxt = turned_west(m + 1)
                    flux = x_faces(here, own, nxt)
                    own = nxt
                turned = [pltpu.roll(f, 1, 1) for f in flux]
                d_x = [f - jnp.where(lane >= 1, p, q) for f, p, q in zip(flux, turned, before)]
                before = turned
                upper = [
                    pltpu.roll(jnp.where(row >= 1, here[k], at(k, rows_b, m)), PAD - 1, 0)
                    for k in range(5)
                ]
                north = faces(here, upper, 2, 1)
                cols = pl.ds(m * LANES, LANES)
                d_y = []
                for k in range(3):
                    south = jnp.where(row < PAD - 1, north[k], prev[k, :, cols])
                    d_y.append(north[k] - pltpu.roll(south, 1, 0))
                    prev[k, :, cols] = north[k]
                if not keep_result:
                    continue
                new = (
                    here[0] - 0.25 * (d_x[0] + d_y[0]),
                    here[3] * (here[1] - 0.25 * (d_x[1] + d_y[2])),
                    here[3] * (here[2] - 0.25 * (d_x[2] + d_y[1])),
                )
                for k in range(3):
                    if last_step:
                        rows_o = pl.ds(pl.multiple_of(a - PAD, PAD), PAD)
                        (out_e, out_u, out_v)[k][rows_o, cols] = new[k]
                    else:
                        cur[k, rows_a, cols] = new[k]

        def body(t, carry):
            advance(t, True)
            return carry

        if last_step:
            advance(0, False)
            lax.fori_loop(1, 1 + cy // PAD, body, 0)
        else:
            lax.fori_loop(0, win // PAD, body, 0)


def local(elevation, flux_x, flux_y, depth, wet_mask, shifts, parent_vals, row_dest, row_coarse,
          edge_owner, edge_panels):
    cy, cx = elevation.shape
    ny, nx = lax.axis_size("ny"), lax.axis_size("nx")
    owners = ny * nx
    n_cols = parent_vals.shape[2]
    n_coarse = cy // RATIO
    sds = jax.ShapeDtypeStruct
    any_ = pl.BlockSpec(memory_space=pl.ANY)
    vm = pl.BlockSpec(memory_space=pltpu.VMEM)
    sm = pl.BlockSpec(memory_space=pltpu.SMEM)

    def whole(ndim, shape):
        return pl.BlockSpec(shape, lambda i: (0,) * ndim)

    last = cx // LANES - 1
    send, tgt, hi_p, lo_p, edge_p = pl.pallas_call(
        functools.partial(prep_kernel, owners),
        out_shape=(
            sds((owners, STEPS * CAP, n_cols), F32),
            sds((owners, 1, LANES), F32),
            sds((cy, 2 * LANES), F32),
            sds((cy, LANES), F32),
            sds((STEPS, cy), F32),
        ),
        grid=(1,),
        in_specs=[
            whole(2, row_dest.shape), whole(2, row_coarse.shape), whole(3, parent_vals.shape),
            pl.BlockSpec((cy, LANES), lambda i: (0, 0)),
            pl.BlockSpec((cy, LANES), lambda i: (0, 0)),
            pl.BlockSpec((cy, LANES), lambda i: (0, 0)),
            pl.BlockSpec((cy, LANES), lambda i: (0, 0)),
            pl.BlockSpec((cy, LANES), lambda i: (0, last)),
            pl.BlockSpec((STEPS, cy, LANES), lambda i: (0, 0, 0)),
            pl.BlockSpec((STEPS, cy, LANES), lambda i: (0, 0, last)),
            whole(2, edge_owner.shape[::-1]), whole(3, edge_panels.shape),
        ],
        name="prep",
    )(row_dest, row_coarse, parent_vals, elevation, flux_x, flux_y, depth, depth, wet_mask,
      wet_mask, edge_owner.T, edge_panels)

    n_halo = 16
    wet_hi = [round_up(w, PAD) for w in WET_HI]
    dma = pltpu.SemaphoreType.DMA
    halos = pl.pallas_call(
        functools.partial(comm_kernel, ny, nx, n_halo),
        out_shape=(
            sds((3, STATE_HI, cx), F32), sds((wet_hi[0], cx), F32),
            *[sds((w, cx), I32) for w in wet_hi],
            sds((PAD, cx), F32), sds((STEPS, PAD, cx), I32),
            sds((PAD + cy + STATE_HI, 2 * LANES), F32),
            sds((PAD + cy + STATE_HI, LANES), F32),
            sds((9, STEPS, n_coarse, n_cols), F32),
            sds((3, nx, STEPS, cy), F32),
        ),
        in_specs=[any_] * 10,
        out_specs=(any_,) * 12,
        scratch_shapes=[
            pltpu.VMEM((owners, STEPS * CAP, n_cols), F32),
            pltpu.VMEM((owners, 1, LANES), F32),
            pltpu.VMEM((STEPS, n_coarse, n_cols), F32),
            dma((2,)), dma((2,)), dma((n_halo,)), dma((n_halo,)), dma((9,)), dma((9,)),
            dma((3,)), dma((3,)), dma((1,)),
        ],
        compiler_params=pltpu.CompilerParams(has_side_effects=True),
        name="exchange",
    )(send, tgt, elevation, flux_x, flux_y, depth, wet_mask, hi_p, lo_p, edge_p)

    width = cx + LANES
    rows = PAD + cy + STATE_HI
    ext_rows = rows + PAD
    win = cy + 2 * PAD
    return pl.pallas_call(
        functools.partial(step_kernel, ny, nx),
        out_shape=(sds((cy, cx), F32),) * 3,
        in_specs=[sm] + [any_] * 17,
        out_specs=(vm,) * 3,
        scratch_shapes=[
            pltpu.VMEM((3, ext_rows, width), F32),
            pltpu.VMEM((ext_rows, width), F32),
            pltpu.VMEM((STEPS, ext_rows, width), I32),
            pltpu.VMEM((rows, 2 * LANES), F32),
            pltpu.VMEM((rows, LANES), F32),
            pltpu.VMEM((3, nx, STEPS, cy), F32),
            pltpu.VMEM((9, STEPS, n_coarse, n_cols), F32),
            pltpu.VMEM((5, win + PAD, width), F32),
            pltpu.VMEM((3, win, width), F32),
            pltpu.VMEM((win, width), F32),
            pltpu.VMEM((2 * n_cols, width), BF16),
            pltpu.VMEM((3, PAD, width), F32),
            dma((32,)),
        ],
        compiler_params=pltpu.CompilerParams(vmem_limit_bytes=56 * 1024 * 1024),
        name="steps",
    )(shifts.T, elevation, flux_x, flux_y, depth, wet_mask, *halos)


def solution(mesh):
    in_specs = (
        P("ny", "nx"),
        P("ny", "nx"),
        P("ny", "nx"),
        P("ny", "nx"),
        P(None, "ny", "nx"),
        P(),
        P(None, ("ny", "nx"), None),
        P(None, ("ny", "nx")),
        P(None, ("ny", "nx")),
        P(None, "ny"),
        P(None, "nx", "ny"),
    )
    out_specs = (P("ny", "nx"), P("ny", "nx"), P("ny", "nx"))
    return jax.shard_map(local, mesh=mesh, in_specs=in_specs, out_specs=out_specs, check_vma=False)
```

```python
import functools

import jax
import jax.numpy as jnp
from jax import lax
from jax.experimental import pallas as pl
from jax.experimental.pallas import tpu as pltpu
from jax.sharding import PartitionSpec as P

RATIO = 9
STEPS = 4
SH = 9
CAP = 8
PAD = 8
LANES = 128
MESH = pl.DeviceIdType.MESH
F32 = jnp.float32
BF16 = jnp.bfloat16
I32 = jnp.int32

STATE_HI = STEPS * (SH + 1)
WET_HI = [SH * (STEPS - 1 - s) + STEPS - s for s in range(STEPS)]
WET_LO = [STEPS - s for s in range(STEPS)]
AUX_HI = [WET_HI[0]] + WET_HI
AUX_LO = [WET_LO[0]] + WET_LO


def starts(widths):
    return [sum(widths[:k]) for k in range(len(widths))]


def round_up(value, unit):
    return -(-value // unit) * unit


def pieces(value):
    high = value.astype(BF16)
    rest = value - high.astype(F32)
    mid = rest.astype(BF16)
    low = (rest - mid.astype(F32)).astype(BF16)
    return high, mid, low


def iota(shape, dim):
    return lax.broadcasted_iota(I32, shape, dim)


def prep_kernel(owners, dest, coarse, vals, e, u, v, d_0, d_1, w_0, w_1, eowner, epanel,
                send, tgt, hi, lo, edge):
    depth, wet = (d_0, d_1), (w_0, w_1)
    rows = dest.shape[1]
    places = owners * CAP
    before = (iota((rows, rows), 0) < iota((rows, rows), 1)).astype(BF16)
    targets = jnp.zeros((owners, LANES), F32)
    for s in range(STEPS):
        d = dest[s : s + 1, :]
        hits = iota((owners, rows), 0) == d
        hits_f = hits.astype(F32)
        earlier = jnp.dot(hits.astype(BF16), before, preferred_element_type=F32)
        rank = jnp.sum(hits_f * earlier, axis=0, keepdims=True).astype(I32)
        place = d * CAP + rank
        pick = (iota((places, rows), 0) == place).astype(BF16)
        total = jnp.zeros((places, vals.shape[2]), F32)
        for piece in pieces(vals[s]):
            total = total + jnp.dot(pick, piece, preferred_element_type=F32)
        send[:, s * CAP : (s + 1) * CAP, :] = total.reshape(owners, CAP, vals.shape[2])
        lane_pick = (iota((LANES, rows), 0) == rank + s * CAP).astype(BF16)
        named = (hits_f * (coarse[s : s + 1, :] + 1).astype(F32)).astype(BF16)
        targets = targets + lax.dot_general(
            named, lane_pick, (((1,), (1,)), ((), ())), preferred_element_type=F32
        )
    for o in range(owners):
        tgt[o] = targets[o : o + 1, :]
    cy = e.shape[0]
    lane = iota((cy, LANES), 1)

    def put(base, tile, at, width):
        moved = pltpu.roll(tile, at % LANES, 1) if at % LANES else tile
        return jnp.where((lane >= at) & (lane < at + width), moved, base)

    first = e[...]
    for k, ref in ((1, u), (2, v)):
        first = put(first, ref[...], k * STATE_HI, STATE_HI)
    hi[:, :LANES] = first
    second = depth[0][...]
    last = jnp.zeros((cy, LANES), F32)
    for k in range(STEPS + 1):
        if k:
            second = put(second, wet[0][k - 1].astype(F32), starts(AUX_HI)[k], AUX_HI[k])
        tile = wet[1][k - 1].astype(F32) if k else depth[1][...]
        at = starts(AUX_LO)[k]
        moved = pltpu.roll(tile, (at + AUX_LO[k]) % LANES, 1)
        last = jnp.where((lane >= at) & (lane < at + AUX_LO[k]), moved, last)
    hi[:, LANES:] = second
    lo[...] = last
    for s in range(STEPS):
        mine = eowner[:, s : s + 1] == lax.axis_index("nx")
        edge[s : s + 1, :] = jnp.where(mine, epanel[s], 0.0)


def comm_kernel(ny, nx, n_halo, send, tgt, e, u, v, depth, wet, hi_p, lo_p, edge_p,
                srs, srd, srw0, srw1, srw2, srw3, nrd, nrw, hi, lo, fc, edges,
                got, got_t, own, a_ssem, a_rsem, h_ssem, h_rsem, f_ssem, f_rsem,
                e_ssem, e_rsem, l_sem):
    y, x = lax.axis_index("ny"), lax.axis_index("nx")
    owners = ny * nx
    me = y * nx + x
    cy = e.shape[0]

    def remote(src, dst, ss, rs, ty, tx):
        return pltpu.make_async_remote_copy(
            src_ref=src, dst_ref=dst, send_sem=ss, recv_sem=rs,
            device_id=(ty, tx), device_id_type=MESH)

    def to_owner(k):
        t = lax.rem(me + k, owners)
        ty, tx = t // nx, lax.rem(t, nx)
        return (remote(send.at[t], got.at[me], a_ssem.at[0], a_rsem.at[0], ty, tx),
                remote(tgt.at[t], got_t.at[me], a_ssem.at[1], a_rsem.at[1], ty, tx))

    def start_owner(k, carry):
        for copy in to_owner(k):
            copy.start()
        return carry

    lax.fori_loop(1, owners, start_owner, 0)
    self_v = pltpu.make_async_copy(send.at[me], got.at[me], a_rsem.at[0])
    self_t = pltpu.make_async_copy(tgt.at[me], got_t.at[me], a_rsem.at[1])
    self_v.start()
    self_t.start()

    def sends_to(dy, dx):
        terms = []
        if dy:
            terms.append(y > 0 if dy < 0 else y < ny - 1)
        if dx:
            terms.append(x > 0 if dx < 0 else x < nx - 1)
        return functools.reduce(jnp.logical_and, terms)

    wet_rows = [srw0, srw1, srw2, srw3]
    plan = [(-1, 0, ref.at[pl.ds(0, STATE_HI)], srs.at[k]) for k, ref in enumerate((e, u, v))]
    plan.append((-1, 0, depth.at[pl.ds(0, srd.shape[0])], srd))
    for s in range(STEPS):
        plan.append((-1, 0, wet.at[s, pl.ds(0, wet_rows[s].shape[0])], wet_rows[s]))
    end = pl.ds(cy - PAD, PAD)
    plan.append((1, 0, depth.at[end], nrd))
    plan.append((1, 0, wet.at[:, end], nrw))
    low_rows = lo.shape[0] - PAD - cy
    plan.append((0, -1, hi_p, hi.at[pl.ds(PAD, cy)]))
    plan.append((0, 1, lo_p, lo.at[pl.ds(PAD, cy)]))
    plan.append((-1, -1, hi_p.at[pl.ds(0, STATE_HI)], hi.at[pl.ds(PAD + cy, STATE_HI)]))
    plan.append((1, -1, hi_p.at[end], hi.at[pl.ds(0, PAD)]))
    plan.append((-1, 1, lo_p.at[pl.ds(0, low_rows)], lo.at[pl.ds(PAD + cy, low_rows)]))
    plan.append((1, 1, lo_p.at[end], lo.at[pl.ds(0, PAD)]))
    assert len(plan) == n_halo
    halos = []
    for k, (dy, dx, src, dst) in enumerate(plan):
        copy = remote(src, dst, h_ssem.at[k], h_rsem.at[k], y + dy, x + dx)
        halos.append((copy, dy, dx))
        pl.when(sends_to(dy, dx))(copy.start)

    for dy in (-1, 0, 1):
        copy = remote(edge_p, edges.at[1 - dy, x], e_ssem.at[1 - dy], e_rsem.at[1 - dy],
                      y + dy, x * 0)
        there = (x > 0) if dy == 0 else sends_to(dy, 0)
        pl.when(there)(copy.start)
    self_e = pltpu.make_async_copy(edge_p, edges.at[1, 0], e_rsem.at[1])
    pl.when(x == 0)(self_e.start)

    pltpu.make_async_copy(got, got, a_rsem.at[0]).wait()
    pltpu.make_async_copy(got_t, got_t, a_rsem.at[1]).wait()
    n_coarse, n_cols = own.shape[1], own.shape[2]
    places = owners * CAP
    named = got_t[:, 0, :].astype(BF16)
    place_owner = iota((owners, places), 1) // CAP
    own_place = place_owner == iota((owners, places), 0)
    slot = iota((LANES, places), 1) - iota((LANES, places), 1) // CAP * CAP
    for s in range(STEPS):
        spread = (iota((LANES, places), 0) == slot + s * CAP).astype(BF16)
        wide = jnp.dot(named, spread, preferred_element_type=F32)
        target = jnp.sum(jnp.where(own_place, wide, 0.0), axis=0, keepdims=True)
        pick = (iota((n_coarse, places), 0).astype(F32) == target - 1.0).astype(BF16)
        values = got[:, s * CAP : (s + 1) * CAP, :].reshape(places, n_cols)
        total = jnp.zeros((n_coarse, n_cols), F32)
        for piece in pieces(values):
            total = total + jnp.dot(pick, piece, preferred_element_type=F32)
        own[s] = total
    half = n_coarse // 2
    self_f = pltpu.make_async_copy(own, fc.at[4], l_sem.at[0])
    self_f.start()
    coarse = []
    for dy in (-1, 0, 1):
        for dx in (-1, 0, 1):
            if dy == 0 and dx == 0:
                continue
            k = (1 - dy) * 3 + (1 - dx)
            part = {-1: pl.ds(0, half), 0: pl.ds(0, n_coarse), 1: pl.ds(half, half)}[dy]
            copy = remote(own.at[:, part], fc.at[k, :, part], f_ssem.at[k], f_rsem.at[k],
                          y + dy, x + dx)
            coarse.append((copy, dy, dx))
            pl.when(sends_to(dy, dx))(copy.start)
    for copy, dy, dx in halos + coarse:
        pl.when(sends_to(-dy, -dx))(copy.wait_recv)
    for dy in (-1, 0, 1):
        whole = edges.at[1 - dy]
        here = (x == 0) if dy == 0 else jnp.logical_and(x == 0, sends_to(-dy, 0))
        pl.when(here)(pltpu.make_async_copy(whole, whole, e_rsem.at[1 - dy]).wait)
    for copy, dy, dx in halos + coarse:
        pl.when(sends_to(dy, dx))(copy.wait_send)
    for dy in (-1, 0, 1):
        copy = remote(edge_p, edges.at[1 - dy, x], e_ssem.at[1 - dy], e_rsem.at[1 - dy],
                      y + dy, x * 0)
        there = (x > 0) if dy == 0 else sends_to(dy, 0)
        pl.when(there)(copy.wait_send)
    self_f.wait()

    def end_owner(k, carry):
        for copy in to_owner(k):
            copy.wait_send()
        return carry

    lax.fori_loop(1, owners, end_owner, 0)


def step_kernel(ny, nx, shifts, e, u, v, depth, wet, srs, srd, srw0, srw1, srw2, srw3,
                nrd, nrw, hi, lo, fc, edges, out_e, out_u, out_v,
                ext, ext_d, ext_w, hi_v, lo_v, edge_v, fc_v, work, cur, force, col_w, prev, sems):
    y, x = lax.axis_index("ny"), lax.axis_index("nx")
    cy, cx = e.shape
    width = ext.shape[2]
    win = cur.shape[1]
    halo = srs.shape[1]
    own_cols = pl.ds(0, cx)
    groups = [[], [], [], [], [], []]
    groups[0] += [(hi, hi_v), (lo, lo_v), (fc, fc_v), (edges, edge_v)]
    for k, ref in enumerate((e, u, v)):
        groups[1].append((ref, ext.at[k, pl.ds(0, cy), own_cols]))
        groups[1].append((srs.at[k], ext.at[k, pl.ds(cy, halo), own_cols]))
    groups[1].append((nrd, ext_d.at[pl.ds(0, PAD), own_cols]))
    groups[1].append((depth, ext_d.at[pl.ds(PAD, cy), own_cols]))
    groups[1].append((srd, ext_d.at[pl.ds(PAD + cy, srd.shape[0]), own_cols]))
    for s, rows in enumerate((srw0, srw1, srw2, srw3)):
        groups[2 + s].append((nrw.at[s], ext_w.at[s, pl.ds(0, PAD), own_cols]))
        groups[2 + s].append((wet.at[s], ext_w.at[s, pl.ds(PAD, cy), own_cols]))
        groups[2 + s].append((rows, ext_w.at[s, pl.ds(PAD + cy, rows.shape[0]), own_cols]))
    copies = []
    count = 0
    for group in groups:
        made = []
        for src, dst in group:
            made.append(pltpu.make_async_copy(src, dst, sems.at[count]))
            made[-1].start()
            count += 1
        copies.append(made)

    def finish(group):
        for copy in copies[group]:
            copy.wait()

    sum_r = [sum([shifts[0, t] for t in range(s, STEPS)], jnp.int32(0)) for s in range(STEPS + 1)]
    sum_c = [sum([shifts[1, t] for t in range(s, STEPS)], jnp.int32(0)) for s in range(STEPS + 1)]

    n_coarse, n_cols = fc.shape[2], fc.shape[3]
    has_y = {-1: y > 0, 0: y >= 0, 1: y < ny - 1}
    has_x = {-1: x > 0, 0: x >= 0, 1: x < nx - 1}
    half = n_coarse // 2

    def weights(fine, which, at, fine_count, coarse_count):
        inner = fine - which * fine_count
        spot = jnp.clip(2 * inner + 1 - RATIO, 0, 2 * RATIO * (coarse_count - 1))
        weight = jnp.maximum(2 * RATIO - jnp.abs(spot - 2 * RATIO * at), 0)
        inside = (inner >= 0) & (inner < fine_count)
        return jnp.where(inside, weight, 0).astype(F32).astype(BF16)

    tiles = width // LANES
    lane = iota((PAD, LANES), 1)
    row = iota((PAD, LANES), 0)

    q = iota((2 * n_cols, LANES), 0)
    at_q = q - jnp.where(q >= n_cols, n_cols, 0)
    which_q = jnp.where(q < n_cols, 0, jnp.where(at_q < n_cols // 2, 1, -1))
    lane_q = iota((2 * n_cols, LANES), 1)
    for k in range(tiles):
        fine = lane_q + k * LANES
        fine = fine - jnp.where(fine >= width - PAD, width, 0)
        col_w[:, k * LANES : (k + 1) * LANES] = weights(fine, which_q, at_q, cx, n_cols)
    finish(0)
    lane_e = iota((n_coarse, n_cols), 1)
    row_e = iota((n_coarse, n_cols), 0)

    def forcing(s):
        q = iota((win, 3 * n_coarse), 1)
        which = (q >= n_coarse).astype(I32) + (q >= 2 * n_coarse).astype(I32) - 1
        fine = iota((win, 3 * n_coarse), 0) - PAD + sum_r[s + 1]
        row_w = weights(fine, which, q - (which + 1) * n_coarse, cy, n_coarse)
        bands = []
        for dy in (-1, 0, 1):
            sides = {}
            for dx in (-1, 0, 1):
                ok = has_y[dy] & has_x[dx]
                block = fc_v[(dy + 1) * 3 + dx + 1, s]
                if dy:
                    ok = ok & ((row_e >= half) if dy < 0 else (row_e < half))
                sides[dx] = jnp.where(ok, block, 0.0)
            beside = jnp.where(lane_e < n_cols // 2, sides[1], sides[-1])
            bands.append(jnp.concatenate([sides[0], beside], axis=1))
        coarse = jnp.concatenate(bands, axis=0)
        section = jnp.zeros((win, 2 * n_cols), F32)
        for piece in pieces(coarse):
            section = section + jnp.dot(row_w, piece, preferred_element_type=F32)
        section = section * (1.0 / (4.0 * RATIO * RATIO))
        total = jnp.zeros((win, width), F32)
        for piece in pieces(section):
            total = total + jnp.dot(piece, col_w[...], preferred_element_type=F32)
        force[...] = total

    rows_here = hi_v.shape[0]
    lane_t = iota((rows_here, LANES), 1)

    def moved(tile, by):
        by = by % LANES
        return pltpu.roll(tile, by, 1) if by else tile

    for k in range(3):
        ext[k, pl.ds(0, cy + halo), cx : cx + LANES] = moved(
            hi_v[pl.ds(PAD, cy + halo), :LANES], -k * STATE_HI)
    high = hi_v[:, LANES:]
    for k in range(STEPS + 1):
        high_k = moved(high, -starts(AUX_HI)[k])
        low_k = moved(lo_v[...], -(starts(AUX_LO)[k] + AUX_LO[k]))
        tile = jnp.where(lane_t < LANES // 2, high_k, low_k)
        if k == 0:
            ext_d[pl.ds(0, rows_here), cx : cx + LANES] = tile
        else:
            ext_w[k - 1, pl.ds(0, rows_here), cx : cx + LANES] = tile.astype(I32)

    edge_sum = jnp.sum(edge_v[...], axis=1)

    def across(pieces_, by):
        turned = [pltpu.roll(f, lax.rem(LANES - by, LANES), 1) for f in pieces_]
        keep = lane < LANES - by
        return [jnp.where(keep, turned[k], turned[(k + 1) % tiles]) for k in range(tiles)]

    def window(load, start, by):
        base = pl.multiple_of(start // PAD * PAD, PAD)
        off = start - base
        turn = lax.rem(PAD - off, PAD)
        upper = row >= off
        out = []
        for k in range(tiles):
            cols = pl.ds(k * LANES, LANES)
            both = jnp.where(upper, load(pl.ds(base, PAD), cols),
                             load(pl.ds(pl.multiple_of(base + PAD, PAD), PAD), cols))
            out.append(pltpu.roll(both, turn, 0))
        return across(out, by)

    def faces(low, up, normal, cross):
        thin = low[3] * up[3]
        n_l, n_h = low[normal], up[normal]
        mass = thin * ((n_l + n_h) - (up[0] - low[0]))
        push = thin * ((low[4] + up[4]) * (up[0] + low[0]) - (n_h - n_l))
        shear = thin * (low[cross] - up[cross])
        return mass, push, shear

    for s in range(STEPS):
        forcing(s)
        if s == 0:
            finish(1)
        finish(2 + s)
        off_r, off_c = sum_r[s + 1], sum_c[s + 1]
        edge_rows = [edge_sum[d, s : s + 1, :] for d in range(3)]

        def fill(t, carry):
            a = pl.multiple_of(t * PAD, PAD)
            here_rows = pl.ds(a, PAD)
            grow = row + (a - PAD) + off_r + y * cy
            row_in = (grow >= 0) & (grow < ny * cy)
            row_ok = row_in & (grow + shifts[0, s] < ny * cy)
            if s == 0:
                fields = [
                    window(lambda r, c: ext[k, r, c], a - PAD + sum_r[0], sum_c[0])
                    for k in range(3)
                ]
            else:
                fields = [
                    [cur[k, here_rows, m * LANES : (m + 1) * LANES] for m in range(tiles)]
                    for k in range(3)
                ]
            wets = window(lambda r, c: ext_w[s, r, c], a + off_r, off_c)
            beds = window(lambda r, c: ext_d[r, c], a + off_r, off_c)
            added = across(
                [force[here_rows, m * LANES : (m + 1) * LANES] for m in range(tiles)], off_c)
            for m in range(tiles):
                valid, inside = row_ok, row_in
                local_col = lane + m * LANES
                if m == tiles - 1:
                    local_col = local_col - jnp.where(local_col >= width - PAD, width, 0)
                gcol = local_col + (x * cx + off_c)
                if (m + 1) * LANES > cx - STEPS * SH:
                    inside = inside & (gcol >= 0) & (gcol < nx * cx)
                    valid = valid & (gcol >= 0) & (gcol + shifts[1, s] < nx * cx)
                e_m = jnp.where(valid, fields[0][m], 0.0) + added[m]
                e_m = jnp.where(inside, e_m, 0.0)
                u_m = jnp.where(valid, fields[1][m], 0.0)
                v_m = jnp.where(valid, fields[2][m], 0.0)
                if s == 0:
                    u_m, v_m = 2.0 * u_m, 2.0 * v_m
                w_m = jnp.where(inside, 0.25 * wets[m].astype(F32), 0.0)
                b_m = jnp.where(inside, 2.0 * beds[m], 0.0)
                if m == tiles - 1:
                    spot = iota((PAD, cy), 0) + (a - PAD) + off_r
                    at = iota((PAD, cy), 1)
                    value = jnp.zeros((PAD, cy), F32)
                    for d in range(3):
                        value = value + jnp.where(at + (d - 1) * cy == spot, edge_rows[d], 0.0)
                    value = jnp.sum(value, axis=1, keepdims=True)
                    ghost = (gcol == -1) & row_in
                    e_m = jnp.where(ghost, value, e_m)
                    w_m = jnp.where(ghost, 0.25, w_m)
                for k, field in enumerate((e_m, u_m, v_m, w_m, b_m)):
                    work[k, m, here_rows, :] = field
            return carry

        lax.fori_loop(0, win // PAD, fill, 0, unroll=2)
        last_step = s == STEPS - 1

        def advance(t, keep_result):
            a = pl.multiple_of(t * PAD, PAD)
            rows_a = pl.ds(a, PAD)
            rows_n = pl.ds(a + 1, PAD)
            rows_f = pl.ds(pl.multiple_of(a + PAD, PAD), PAD)
            rows_s = pl.ds(a + PAD - 1, PAD)

            def at(k, rows_, m):
                return work[k, m, rows_, :]

            def turned_west(m):
                return [pltpu.roll(at(k, rows_a, m), LANES - 1, 1) for k in range(5)]

            def x_faces(here, own, nxt):
                east = [jnp.where(lane < LANES - 1, p, q) for p, q in zip(own, nxt)]
                return faces(here, east, 1, 2)

            n_out = tiles - 1 if last_step else tiles
            first = turned_west(0)
            tail = [at(k, rows_a, tiles - 1) for k in range(5)]
            flux_tail = x_faces(tail, turned_west(tiles - 1), first)
            before = [pltpu.roll(f, 1, 1) for f in flux_tail]
            own = first
            for m in range(n_out):
                here = [at(k, rows_a, m) for k in range(5)]
                if m == tiles - 1:
                    flux = flux_tail
                else:
                    nxt = turned_west(m + 1)
                    flux = x_faces(here, own, nxt)
                    own = nxt
                turned = [pltpu.roll(f, 1, 1) for f in flux]
                d_x = [f - jnp.where(lane >= 1, p, q) for f, p, q in zip(flux, turned, before)]
                before = turned
                north = faces(here, [at(k, rows_n, m) for k in range(5)], 2, 1)
                cols = pl.ds(m * LANES, LANES)
                d_y = []
                for k in range(3):
                    prev[k, m, rows_f, :] = north[k]
                    d_y.append(north[k] - prev[k, m, rows_s, :])
                if not keep_result:
                    continue
                scale = (2.0 if last_step else 4.0) * here[3]
                new = (
                    here[0] - (d_x[0] + d_y[0]),
                    scale * (here[1] - (d_x[1] + d_y[2])),
                    scale * (here[2] - (d_x[2] + d_y[1])),
                )
                for k in range(3):
                    if last_step:
                        rows_o = pl.ds(pl.multiple_of(a - PAD, PAD), PAD)
                        (out_e, out_u, out_v)[k][rows_o, cols] = new[k]
                    else:
                        cur[k, rows_a, cols] = new[k]

        def body(t, carry):
            advance(t, True)
            return carry

        if last_step:
            advance(0, False)
            lax.fori_loop(1, 1 + cy // PAD, body, 0)
        else:
            lax.fori_loop(0, win // PAD, body, 0)


def local(elevation, flux_x, flux_y, depth, wet_mask, shifts, parent_vals, row_dest, row_coarse,
          edge_owner, edge_panels):
    cy, cx = elevation.shape
    ny, nx = lax.axis_size("ny"), lax.axis_size("nx")
    owners = ny * nx
    n_cols = parent_vals.shape[2]
    n_coarse = cy // RATIO
    sds = jax.ShapeDtypeStruct
    any_ = pl.BlockSpec(memory_space=pl.ANY)
    vm = pl.BlockSpec(memory_space=pltpu.VMEM)
    sm = pl.BlockSpec(memory_space=pltpu.SMEM)

    def whole(ndim, shape):
        return pl.BlockSpec(shape, lambda i: (0,) * ndim)

    last = cx // LANES - 1
    send, tgt, hi_p, lo_p, edge_p = pl.pallas_call(
        functools.partial(prep_kernel, owners),
        out_shape=(
            sds((owners, STEPS * CAP, n_cols), F32),
            sds((owners, 1, LANES), F32),
            sds((cy, 2 * LANES), F32),
            sds((cy, LANES), F32),
            sds((STEPS, cy), F32),
        ),
        grid=(1,),
        in_specs=[
            whole(2, row_dest.shape), whole(2, row_coarse.shape), whole(3, parent_vals.shape),
            pl.BlockSpec((cy, LANES), lambda i: (0, 0)),
            pl.BlockSpec((cy, LANES), lambda i: (0, 0)),
            pl.BlockSpec((cy, LANES), lambda i: (0, 0)),
            pl.BlockSpec((cy, LANES), lambda i: (0, 0)),
            pl.BlockSpec((cy, LANES), lambda i: (0, last)),
            pl.BlockSpec((STEPS, cy, LANES), lambda i: (0, 0, 0)),
            pl.BlockSpec((STEPS, cy, LANES), lambda i: (0, 0, last)),
            whole(2, edge_owner.shape[::-1]), whole(3, edge_panels.shape),
        ],
        name="prep",
    )(row_dest, row_coarse, parent_vals, elevation, flux_x, flux_y, depth, depth, wet_mask,
      wet_mask, edge_owner.T, edge_panels)

    n_halo = 16
    wet_hi = [round_up(w, PAD) for w in WET_HI]
    dma = pltpu.SemaphoreType.DMA
    halos = pl.pallas_call(
        functools.partial(comm_kernel, ny, nx, n_halo),
        out_shape=(
            sds((3, STATE_HI, cx), F32), sds((wet_hi[0], cx), F32),
            *[sds((w, cx), I32) for w in wet_hi],
            sds((PAD, cx), F32), sds((STEPS, PAD, cx), I32),
            sds((PAD + cy + STATE_HI, 2 * LANES), F32),
            sds((PAD + cy + STATE_HI, LANES), F32),
            sds((9, STEPS, n_coarse, n_cols), F32),
            sds((3, nx, STEPS, cy), F32),
        ),
        in_specs=[any_] * 10,
        out_specs=(any_,) * 12,
        scratch_shapes=[
            pltpu.VMEM((owners, STEPS * CAP, n_cols), F32),
            pltpu.VMEM((owners, 1, LANES), F32),
            pltpu.VMEM((STEPS, n_coarse, n_cols), F32),
            dma((2,)), dma((2,)), dma((n_halo,)), dma((n_halo,)), dma((9,)), dma((9,)),
            dma((3,)), dma((3,)), dma((1,)),
        ],
        compiler_params=pltpu.CompilerParams(has_side_effects=True),
        name="exchange",
    )(send, tgt, elevation, flux_x, flux_y, depth, wet_mask, hi_p, lo_p, edge_p)

    width = cx + LANES
    rows = PAD + cy + STATE_HI
    ext_rows = rows + PAD
    win = cy + 2 * PAD
    return pl.pallas_call(
        functools.partial(step_kernel, ny, nx),
        out_shape=(sds((cy, cx), F32),) * 3,
        in_specs=[sm] + [any_] * 17,
        out_specs=(vm,) * 3,
        scratch_shapes=[
            pltpu.VMEM((3, ext_rows, width), F32),
            pltpu.VMEM((ext_rows, width), F32),
            pltpu.VMEM((STEPS, ext_rows, width), I32),
            pltpu.VMEM((rows, 2 * LANES), F32),
            pltpu.VMEM((rows, LANES), F32),
            pltpu.VMEM((3, nx, STEPS, cy), F32),
            pltpu.VMEM((9, STEPS, n_coarse, n_cols), F32),
            pltpu.VMEM((5, width // LANES, win + PAD, LANES), F32),
            pltpu.VMEM((3, win, width), F32),
            pltpu.VMEM((win, width), F32),
            pltpu.VMEM((2 * n_cols, width), BF16),
            pltpu.VMEM((3, width // LANES, win + PAD, LANES), F32),
            dma((32,)),
        ],
        compiler_params=pltpu.CompilerParams(vmem_limit_bytes=56 * 1024 * 1024),
        name="steps",
    )(shifts.T, elevation, flux_x, flux_y, depth, wet_mask, *halos)


def solution(mesh):
    in_specs = (
        P("ny", "nx"),
        P("ny", "nx"),
        P("ny", "nx"),
        P("ny", "nx"),
        P(None, "ny", "nx"),
        P(),
        P(None, ("ny", "nx"), None),
        P(None, ("ny", "nx")),
        P(None, ("ny", "nx")),
        P(None, "ny"),
        P(None, "nx", "ny"),
    )
    out_specs = (P("ny", "nx"), P("ny", "nx"), P("ny", "nx"))
    return jax.shard_map(local, mesh=mesh, in_specs=in_specs, out_specs=out_specs, check_vma=False)
```

```python
import functools

import jax
import jax.numpy as jnp
from jax import lax
from jax.experimental import pallas as pl
from jax.experimental.pallas import tpu as pltpu
from jax.sharding import PartitionSpec as P

RATIO = 9
STEPS = 4
SH = 9
CAP = 8
PAD = 8
LANES = 128
MESH = pl.DeviceIdType.MESH
F32 = jnp.float32
BF16 = jnp.bfloat16
I32 = jnp.int32

STATE_HI = STEPS * (SH + 1)
WET_HI = [SH * (STEPS - 1 - s) + STEPS - s for s in range(STEPS)]
WET_LO = [STEPS - s for s in range(STEPS)]
AUX_HI = [WET_HI[0]] + WET_HI
AUX_LO = [WET_LO[0]] + WET_LO


def starts(widths):
    return [sum(widths[:k]) for k in range(len(widths))]


def round_up(value, unit):
    return -(-value // unit) * unit


def pieces(value):
    high = value.astype(BF16)
    rest = value - high.astype(F32)
    mid = rest.astype(BF16)
    low = (rest - mid.astype(F32)).astype(BF16)
    return high, mid, low


def iota(shape, dim):
    return lax.broadcasted_iota(I32, shape, dim)


def prep_kernel(owners, dest, coarse, vals, e, u, v, d_0, d_1, w_0, w_1, eowner, epanel,
                send, tgt, hi, lo, edge):
    depth, wet = (d_0, d_1), (w_0, w_1)
    rows = dest.shape[1]
    places = owners * CAP
    before = (iota((rows, rows), 0) < iota((rows, rows), 1)).astype(BF16)
    targets = jnp.zeros((owners, LANES), F32)
    for s in range(STEPS):
        d = dest[s : s + 1, :]
        hits = iota((owners, rows), 0) == d
        hits_f = hits.astype(F32)
        earlier = jnp.dot(hits.astype(BF16), before, preferred_element_type=F32)
        rank = jnp.sum(hits_f * earlier, axis=0, keepdims=True).astype(I32)
        place = d * CAP + rank
        pick = (iota((places, rows), 0) == place).astype(BF16)
        total = jnp.zeros((places, vals.shape[2]), F32)
        for piece in pieces(vals[s]):
            total = total + jnp.dot(pick, piece, preferred_element_type=F32)
        send[:, s * CAP : (s + 1) * CAP, :] = total.reshape(owners, CAP, vals.shape[2])
        lane_pick = (iota((LANES, rows), 0) == rank + s * CAP).astype(BF16)
        named = (hits_f * (coarse[s : s + 1, :] + 1).astype(F32)).astype(BF16)
        targets = targets + lax.dot_general(
            named, lane_pick, (((1,), (1,)), ((), ())), preferred_element_type=F32
        )
    for o in range(owners):
        tgt[o] = targets[o : o + 1, :]
    cy = e.shape[0]
    lane = iota((cy, LANES), 1)

    def put(base, tile, at, width):
        moved = pltpu.roll(tile, at % LANES, 1) if at % LANES else tile
        return jnp.where((lane >= at) & (lane < at + width), moved, base)

    first = e[...]
    for k, ref in ((1, u), (2, v)):
        first = put(first, ref[...], k * STATE_HI, STATE_HI)
    hi[:, :LANES] = first
    second = depth[0][...]
    last = jnp.zeros((cy, LANES), F32)
    for k in range(STEPS + 1):
        if k:
            second = put(second, wet[0][k - 1].astype(F32), starts(AUX_HI)[k], AUX_HI[k])
        tile = wet[1][k - 1].astype(F32) if k else depth[1][...]
        at = starts(AUX_LO)[k]
        moved = pltpu.roll(tile, (at + AUX_LO[k]) % LANES, 1)
        last = jnp.where((lane >= at) & (lane < at + AUX_LO[k]), moved, last)
    hi[:, LANES:] = second
    lo[...] = last
    for s in range(STEPS):
        mine = eowner[:, s : s + 1] == lax.axis_index("nx")
        edge[s : s + 1, :] = jnp.where(mine, epanel[s], 0.0)


def comm_kernel(ny, nx, n_halo, dest, coarse_in, vals, e_0, u_0, v_0, d_0, d_1, w_0, w_1, eowner,
                epanel, e, u, v, depth, wet,
                srs, srd, srw0, srw1, srw2, srw3, nrd, nrw, hi, lo, fc, edges,
                send, tgt, hi_p, lo_p, edge_p, got, got_t, own, a_ssem, a_rsem, h_ssem, h_rsem, f_ssem, f_rsem,
                e_ssem, e_rsem, l_sem):
    y, x = lax.axis_index("ny"), lax.axis_index("nx")
    owners = ny * nx
    me = y * nx + x
    cy = e.shape[0]

    def remote(src, dst, ss, rs, ty, tx):
        return pltpu.make_async_remote_copy(
            src_ref=src, dst_ref=dst, send_sem=ss, recv_sem=rs,
            device_id=(ty, tx), device_id_type=MESH)

    def to_owner(k):
        t = lax.rem(me + k, owners)
        ty, tx = t // nx, lax.rem(t, nx)
        return (remote(send.at[t], got.at[me], a_ssem.at[0], a_rsem.at[0], ty, tx),
                remote(tgt.at[t], got_t.at[me], a_ssem.at[1], a_rsem.at[1], ty, tx))

    def start_owner(k, carry):
        for copy in to_owner(k):
            copy.start()
        return carry

    def sends_to(dy, dx):
        terms = []
        if dy:
            terms.append(y > 0 if dy < 0 else y < ny - 1)
        if dx:
            terms.append(x > 0 if dx < 0 else x < nx - 1)
        return functools.reduce(jnp.logical_and, terms)

    wet_rows = [srw0, srw1, srw2, srw3]
    plan = [(-1, 0, ref.at[pl.ds(0, STATE_HI)], srs.at[k]) for k, ref in enumerate((e, u, v))]
    plan.append((-1, 0, depth.at[pl.ds(0, srd.shape[0])], srd))
    for s in range(STEPS):
        plan.append((-1, 0, wet.at[s, pl.ds(0, wet_rows[s].shape[0])], wet_rows[s]))
    end = pl.ds(cy - PAD, PAD)
    plan.append((1, 0, depth.at[end], nrd))
    plan.append((1, 0, wet.at[:, end], nrw))
    low_rows = lo.shape[0] - PAD - cy
    plan.append((0, -1, hi_p, hi.at[pl.ds(PAD, cy)]))
    plan.append((0, 1, lo_p, lo.at[pl.ds(PAD, cy)]))
    plan.append((-1, -1, hi_p.at[pl.ds(0, STATE_HI)], hi.at[pl.ds(PAD + cy, STATE_HI)]))
    plan.append((1, -1, hi_p.at[end], hi.at[pl.ds(0, PAD)]))
    plan.append((-1, 1, lo_p.at[pl.ds(0, low_rows)], lo.at[pl.ds(PAD + cy, low_rows)]))
    plan.append((1, 1, lo_p.at[end], lo.at[pl.ds(0, PAD)]))
    assert len(plan) == n_halo
    halos = []
    for k, (dy, dx, src, dst) in enumerate(plan):
        if dx and not plan[k - 1][1]:
            prep_kernel(owners, dest, coarse_in, vals, e_0, u_0, v_0, d_0, d_1, w_0, w_1, eowner,
                        epanel, send, tgt, hi_p, lo_p, edge_p)
            lax.fori_loop(1, owners, start_owner, 0)
            self_v = pltpu.make_async_copy(send.at[me], got.at[me], a_rsem.at[0])
            self_t = pltpu.make_async_copy(tgt.at[me], got_t.at[me], a_rsem.at[1])
            self_v.start()
            self_t.start()
        copy = remote(src, dst, h_ssem.at[k], h_rsem.at[k], y + dy, x + dx)
        halos.append((copy, dy, dx))
        pl.when(sends_to(dy, dx))(copy.start)

    for dy in (-1, 0, 1):
        copy = remote(edge_p, edges.at[1 - dy, x], e_ssem.at[1 - dy], e_rsem.at[1 - dy],
                      y + dy, x * 0)
        there = (x > 0) if dy == 0 else sends_to(dy, 0)
        pl.when(there)(copy.start)
    self_e = pltpu.make_async_copy(edge_p, edges.at[1, 0], e_rsem.at[1])
    pl.when(x == 0)(self_e.start)

    pltpu.make_async_copy(got, got, a_rsem.at[0]).wait()
    pltpu.make_async_copy(got_t, got_t, a_rsem.at[1]).wait()
    n_coarse, n_cols = own.shape[1], own.shape[2]
    places = owners * CAP
    named = got_t[:, 0, :].astype(BF16)
    place_owner = iota((owners, places), 1) // CAP
    own_place = place_owner == iota((owners, places), 0)
    slot = iota((LANES, places), 1) - iota((LANES, places), 1) // CAP * CAP
    for s in range(STEPS):
        spread = (iota((LANES, places), 0) == slot + s * CAP).astype(BF16)
        wide = jnp.dot(named, spread, preferred_element_type=F32)
        target = jnp.sum(jnp.where(own_place, wide, 0.0), axis=0, keepdims=True)
        pick = (iota((n_coarse, places), 0).astype(F32) == target - 1.0).astype(BF16)
        values = got[:, s * CAP : (s + 1) * CAP, :].reshape(places, n_cols)
        total = jnp.zeros((n_coarse, n_cols), F32)
        for piece in pieces(values):
            total = total + jnp.dot(pick, piece, preferred_element_type=F32)
        own[s] = total
    half = n_coarse // 2
    self_f = pltpu.make_async_copy(own, fc.at[4], l_sem.at[0])
    self_f.start()
    coarse = []
    for dy in (-1, 0, 1):
        for dx in (-1, 0, 1):
            if dy == 0 and dx == 0:
                continue
            k = (1 - dy) * 3 + (1 - dx)
            part = {-1: pl.ds(0, half), 0: pl.ds(0, n_coarse), 1: pl.ds(half, half)}[dy]
            copy = remote(own.at[:, part], fc.at[k, :, part], f_ssem.at[k], f_rsem.at[k],
                          y + dy, x + dx)
            coarse.append((copy, dy, dx))
            pl.when(sends_to(dy, dx))(copy.start)
    for copy, dy, dx in halos + coarse:
        pl.when(sends_to(-dy, -dx))(copy.wait_recv)
    for dy in (-1, 0, 1):
        whole = edges.at[1 - dy]
        here = (x == 0) if dy == 0 else jnp.logical_and(x == 0, sends_to(-dy, 0))
        pl.when(here)(pltpu.make_async_copy(whole, whole, e_rsem.at[1 - dy]).wait)
    for copy, dy, dx in halos + coarse:
        pl.when(sends_to(dy, dx))(copy.wait_send)
    for dy in (-1, 0, 1):
        copy = remote(edge_p, edges.at[1 - dy, x], e_ssem.at[1 - dy], e_rsem.at[1 - dy],
                      y + dy, x * 0)
        there = (x > 0) if dy == 0 else sends_to(dy, 0)
        pl.when(there)(copy.wait_send)
    self_f.wait()

    def end_owner(k, carry):
        for copy in to_owner(k):
            copy.wait_send()
        return carry

    lax.fori_loop(1, owners, end_owner, 0)


def step_kernel(ny, nx, shifts, e, u, v, depth, wet, srs, srd, srw0, srw1, srw2, srw3,
                nrd, nrw, hi, lo, fc, edges, out_e, out_u, out_v,
                ext, ext_d, ext_w, hi_v, lo_v, edge_v, fc_v, work, cur, force, col_w, prev, sems):
    y, x = lax.axis_index("ny"), lax.axis_index("nx")
    cy, cx = e.shape
    width = ext.shape[2]
    win = cur.shape[1]
    halo = srs.shape[1]
    own_cols = pl.ds(0, cx)
    groups = [[], [], [], [], [], []]
    groups[0] += [(hi, hi_v), (lo, lo_v), (fc, fc_v), (edges, edge_v)]
    for k, ref in enumerate((e, u, v)):
        groups[1].append((ref, ext.at[k, pl.ds(0, cy), own_cols]))
        groups[1].append((srs.at[k], ext.at[k, pl.ds(cy, halo), own_cols]))
    groups[1].append((nrd, ext_d.at[pl.ds(0, PAD), own_cols]))
    groups[1].append((depth, ext_d.at[pl.ds(PAD, cy), own_cols]))
    groups[1].append((srd, ext_d.at[pl.ds(PAD + cy, srd.shape[0]), own_cols]))
    for s, rows in enumerate((srw0, srw1, srw2, srw3)):
        groups[2 + s].append((nrw.at[s], ext_w.at[s, pl.ds(0, PAD), own_cols]))
        groups[2 + s].append((wet.at[s], ext_w.at[s, pl.ds(PAD, cy), own_cols]))
        groups[2 + s].append((rows, ext_w.at[s, pl.ds(PAD + cy, rows.shape[0]), own_cols]))
    copies = []
    count = 0
    for group in groups:
        made = []
        for src, dst in group:
            made.append(pltpu.make_async_copy(src, dst, sems.at[count]))
            made[-1].start()
            count += 1
        copies.append(made)

    def finish(group):
        for copy in copies[group]:
            copy.wait()

    sum_r = [sum([shifts[0, t] for t in range(s, STEPS)], jnp.int32(0)) for s in range(STEPS + 1)]
    sum_c = [sum([shifts[1, t] for t in range(s, STEPS)], jnp.int32(0)) for s in range(STEPS + 1)]

    n_coarse, n_cols = fc.shape[2], fc.shape[3]
    has_y = {-1: y > 0, 0: y >= 0, 1: y < ny - 1}
    has_x = {-1: x > 0, 0: x >= 0, 1: x < nx - 1}
    half = n_coarse // 2

    def weights(fine, which, at, fine_count, coarse_count):
        inner = fine - which * fine_count
        spot = jnp.clip(2 * inner + 1 - RATIO, 0, 2 * RATIO * (coarse_count - 1))
        weight = jnp.maximum(2 * RATIO - jnp.abs(spot - 2 * RATIO * at), 0)
        inside = (inner >= 0) & (inner < fine_count)
        return jnp.where(inside, weight, 0).astype(F32).astype(BF16)

    tiles = width // LANES
    lane = iota((PAD, LANES), 1)
    row = iota((PAD, LANES), 0)

    q = iota((2 * n_cols, LANES), 0)
    at_q = q - jnp.where(q >= n_cols, n_cols, 0)
    which_q = jnp.where(q < n_cols, 0, jnp.where(at_q < n_cols // 2, 1, -1))
    lane_q = iota((2 * n_cols, LANES), 1)
    for k in range(tiles):
        fine = lane_q + k * LANES
        fine = fine - jnp.where(fine >= width - PAD, width, 0)
        col_w[:, k * LANES : (k + 1) * LANES] = weights(fine, which_q, at_q, cx, n_cols)
    finish(0)
    lane_e = iota((n_coarse, n_cols), 1)
    row_e = iota((n_coarse, n_cols), 0)

    def forcing(s):
        q = iota((win, 3 * n_coarse), 1)
        which = (q >= n_coarse).astype(I32) + (q >= 2 * n_coarse).astype(I32) - 1
        fine = iota((win, 3 * n_coarse), 0) - PAD + sum_r[s + 1]
        row_w = weights(fine, which, q - (which + 1) * n_coarse, cy, n_coarse)
        bands = []
        for dy in (-1, 0, 1):
            sides = {}
            for dx in (-1, 0, 1):
                ok = has_y[dy] & has_x[dx]
                block = fc_v[(dy + 1) * 3 + dx + 1, s]
                if dy:
                    ok = ok & ((row_e >= half) if dy < 0 else (row_e < half))
                sides[dx] = jnp.where(ok, block, 0.0)
            beside = jnp.where(lane_e < n_cols // 2, sides[1], sides[-1])
            bands.append(jnp.concatenate([sides[0], beside], axis=1))
        coarse = jnp.concatenate(bands, axis=0)
        section = jnp.zeros((win, 2 * n_cols), F32)
        for piece in pieces(coarse):
            section = section + jnp.dot(row_w, piece, preferred_element_type=F32)
        section = section * (1.0 / (4.0 * RATIO * RATIO))
        total = jnp.zeros((win, width), F32)
        for piece in pieces(section):
            total = total + jnp.dot(piece, col_w[...], preferred_element_type=F32)
        force[...] = total

    rows_here = hi_v.shape[0]
    lane_t = iota((rows_here, LANES), 1)

    def moved(tile, by):
        by = by % LANES
        return pltpu.roll(tile, by, 1) if by else tile

    for k in range(3):
        ext[k, pl.ds(0, cy + halo), cx : cx + LANES] = moved(
            hi_v[pl.ds(PAD, cy + halo), :LANES], -k * STATE_HI)
    high = hi_v[:, LANES:]
    for k in range(STEPS + 1):
        high_k = moved(high, -starts(AUX_HI)[k])
        low_k = moved(lo_v[...], -(starts(AUX_LO)[k] + AUX_LO[k]))
        tile = jnp.where(lane_t < LANES // 2, high_k, low_k)
        if k == 0:
            ext_d[pl.ds(0, rows_here), cx : cx + LANES] = tile
        else:
            ext_w[k - 1, pl.ds(0, rows_here), cx : cx + LANES] = tile.astype(I32)

    edge_sum = jnp.sum(edge_v[...], axis=1)

    def across(pieces_, by):
        turned = [pltpu.roll(f, lax.rem(LANES - by, LANES), 1) for f in pieces_]
        keep = lane < LANES - by
        return [jnp.where(keep, turned[k], turned[(k + 1) % tiles]) for k in range(tiles)]

    def window(load, start, by):
        base = pl.multiple_of(start // PAD * PAD, PAD)
        off = start - base
        turn = lax.rem(PAD - off, PAD)
        upper = row >= off
        out = []
        for k in range(tiles):
            cols = pl.ds(k * LANES, LANES)
            both = jnp.where(upper, load(pl.ds(base, PAD), cols),
                             load(pl.ds(pl.multiple_of(base + PAD, PAD), PAD), cols))
            out.append(pltpu.roll(both, turn, 0))
        return across(out, by)

    def faces(low, up, normal, cross):
        thin = low[3] * up[3]
        n_l, n_h = low[normal], up[normal]
        mass = thin * ((n_l + n_h) - (up[0] - low[0]))
        push = thin * ((low[4] + up[4]) * (up[0] + low[0]) - (n_h - n_l))
        shear = thin * (low[cross] - up[cross])
        return mass, push, shear

    for s in range(STEPS):
        forcing(s)
        if s == 0:
            finish(1)
        finish(2 + s)
        off_r, off_c = sum_r[s + 1], sum_c[s + 1]
        edge_rows = [edge_sum[d, s : s + 1, :] for d in range(3)]

        def fill(t, carry):
            a = pl.multiple_of(t * PAD, PAD)
            here_rows = pl.ds(a, PAD)
            grow = row + (a - PAD) + off_r + y * cy
            row_in = (grow >= 0) & (grow < ny * cy)
            row_ok = row_in & (grow + shifts[0, s] < ny * cy)
            if s == 0:
                fields = [
                    window(lambda r, c: ext[k, r, c], a - PAD + sum_r[0], sum_c[0])
                    for k in range(3)
                ]
            else:
                fields = [
                    [cur[k, here_rows, m * LANES : (m + 1) * LANES] for m in range(tiles)]
                    for k in range(3)
                ]
            wets = window(lambda r, c: ext_w[s, r, c], a + off_r, off_c)
            beds = window(lambda r, c: ext_d[r, c], a + off_r, off_c)
            added = across(
                [force[here_rows, m * LANES : (m + 1) * LANES] for m in range(tiles)], off_c)
            for m in range(tiles):
                valid, inside = row_ok, row_in
                local_col = lane + m * LANES
                if m == tiles - 1:
                    local_col = local_col - jnp.where(local_col >= width - PAD, width, 0)
                gcol = local_col + (x * cx + off_c)
                if (m + 1) * LANES > cx - STEPS * SH:
                    inside = inside & (gcol >= 0) & (gcol < nx * cx)
                    valid = valid & (gcol >= 0) & (gcol + shifts[1, s] < nx * cx)
                e_m = jnp.where(valid, fields[0][m], 0.0) + added[m]
                e_m = jnp.where(inside, e_m, 0.0)
                u_m = jnp.where(valid, fields[1][m], 0.0)
                v_m = jnp.where(valid, fields[2][m], 0.0)
                if s == 0:
                    u_m, v_m = 2.0 * u_m, 2.0 * v_m
                w_m = jnp.where(inside, 0.25 * wets[m].astype(F32), 0.0)
                b_m = jnp.where(inside, 2.0 * beds[m], 0.0)
                if m == tiles - 1:
                    spot = iota((PAD, cy), 0) + (a - PAD) + off_r
                    at = iota((PAD, cy), 1)
                    value = jnp.zeros((PAD, cy), F32)
                    for d in range(3):
                        value = value + jnp.where(at + (d - 1) * cy == spot, edge_rows[d], 0.0)
                    value = jnp.sum(value, axis=1, keepdims=True)
                    ghost = (gcol == -1) & row_in
                    e_m = jnp.where(ghost, value, e_m)
                    w_m = jnp.where(ghost, 0.25, w_m)
                for k, field in enumerate((e_m, u_m, v_m, w_m, b_m)):
                    work[k, m, here_rows, :] = field
            return carry

        lax.fori_loop(0, win // PAD, fill, 0, unroll=2)
        last_step = s == STEPS - 1

        def advance(t, keep_result):
            a = pl.multiple_of(t * PAD, PAD)
            rows_a = pl.ds(a, PAD)
            rows_n = pl.ds(a + 1, PAD)
            rows_f = pl.ds(pl.multiple_of(a + PAD, PAD), PAD)
            rows_s = pl.ds(a + PAD - 1, PAD)

            def at(k, rows_, m):
                return work[k, m, rows_, :]

            def turned_west(m):
                return [pltpu.roll(at(k, rows_a, m), LANES - 1, 1) for k in range(5)]

            def x_faces(here, own, nxt):
                east = [jnp.where(lane < LANES - 1, p, q) for p, q in zip(own, nxt)]
                return faces(here, east, 1, 2)

            n_out = tiles - 1 if last_step else tiles
            first = turned_west(0)
            tail = [at(k, rows_a, tiles - 1) for k in range(5)]
            flux_tail = x_faces(tail, turned_west(tiles - 1), first)
            before = [pltpu.roll(f, 1, 1) for f in flux_tail]
            own = first
            for m in range(n_out):
                here = [at(k, rows_a, m) for k in range(5)]
                if m == tiles - 1:
                    flux = flux_tail
                else:
                    nxt = turned_west(m + 1)
                    flux = x_faces(here, own, nxt)
                    own = nxt
                turned = [pltpu.roll(f, 1, 1) for f in flux]
                d_x = [f - jnp.where(lane >= 1, p, q) for f, p, q in zip(flux, turned, before)]
                before = turned
                north = faces(here, [at(k, rows_n, m) for k in range(5)], 2, 1)
                cols = pl.ds(m * LANES, LANES)
                d_y = []
                for k in range(3):
                    prev[k, m, rows_f, :] = north[k]
                    d_y.append(north[k] - prev[k, m, rows_s, :])
                if not keep_result:
                    continue
                scale = (2.0 if last_step else 4.0) * here[3]
                new = (
                    here[0] - (d_x[0] + d_y[0]),
                    scale * (here[1] - (d_x[1] + d_y[2])),
                    scale * (here[2] - (d_x[2] + d_y[1])),
                )
                for k in range(3):
                    if last_step:
                        rows_o = pl.ds(pl.multiple_of(a - PAD, PAD), PAD)
                        (out_e, out_u, out_v)[k][rows_o, cols] = new[k]
                    else:
                        cur[k, rows_a, cols] = new[k]

        def body(t, carry):
            advance(t, True)
            return carry

        if last_step:
            advance(0, False)
            lax.fori_loop(1, 1 + cy // PAD, body, 0)
        else:
            lax.fori_loop(0, win // PAD, body, 0)


def local(elevation, flux_x, flux_y, depth, wet_mask, shifts, parent_vals, row_dest, row_coarse,
          edge_owner, edge_panels):
    cy, cx = elevation.shape
    ny, nx = lax.axis_size("ny"), lax.axis_size("nx")
    owners = ny * nx
    n_cols = parent_vals.shape[2]
    n_coarse = cy // RATIO
    sds = jax.ShapeDtypeStruct
    any_ = pl.BlockSpec(memory_space=pl.ANY)
    vm = pl.BlockSpec(memory_space=pltpu.VMEM)
    sm = pl.BlockSpec(memory_space=pltpu.SMEM)

    def whole(ndim, shape):
        return pl.BlockSpec(shape, lambda i: (0,) * ndim)

    last = cx // LANES - 1
    n_halo = 16
    wet_hi = [round_up(w, PAD) for w in WET_HI]
    dma = pltpu.SemaphoreType.DMA
    halos = pl.pallas_call(
        functools.partial(comm_kernel, ny, nx, n_halo),
        out_shape=(
            sds((3, STATE_HI, cx), F32), sds((wet_hi[0], cx), F32),
            *[sds((w, cx), I32) for w in wet_hi],
            sds((PAD, cx), F32), sds((STEPS, PAD, cx), I32),
            sds((PAD + cy + STATE_HI, 2 * LANES), F32),
            sds((PAD + cy + STATE_HI, LANES), F32),
            sds((9, STEPS, n_coarse, n_cols), F32),
            sds((3, nx, STEPS, cy), F32),
        ),
        grid=(1,),
        in_specs=[
            whole(2, row_dest.shape), whole(2, row_coarse.shape), whole(3, parent_vals.shape),
            pl.BlockSpec((cy, LANES), lambda i: (0, 0)),
            pl.BlockSpec((cy, LANES), lambda i: (0, 0)),
            pl.BlockSpec((cy, LANES), lambda i: (0, 0)),
            pl.BlockSpec((cy, LANES), lambda i: (0, 0)),
            pl.BlockSpec((cy, LANES), lambda i: (0, last)),
            pl.BlockSpec((STEPS, cy, LANES), lambda i: (0, 0, 0)),
            pl.BlockSpec((STEPS, cy, LANES), lambda i: (0, 0, last)),
            whole(2, edge_owner.shape[::-1]), whole(3, edge_panels.shape),
        ] + [any_] * 5,
        out_specs=(any_,) * 12,
        scratch_shapes=[
            pltpu.VMEM((owners, STEPS * CAP, n_cols), F32),
            pltpu.VMEM((owners, 1, LANES), F32),
            pltpu.VMEM((cy, 2 * LANES), F32),
            pltpu.VMEM((cy, LANES), F32),
            pltpu.VMEM((STEPS, cy), F32),
            pltpu.VMEM((owners, STEPS * CAP, n_cols), F32),
            pltpu.VMEM((owners, 1, LANES), F32),
            pltpu.VMEM((STEPS, n_coarse, n_cols), F32),
            dma((2,)), dma((2,)), dma((n_halo,)), dma((n_halo,)), dma((9,)), dma((9,)),
            dma((3,)), dma((3,)), dma((1,)),
        ],
        compiler_params=pltpu.CompilerParams(has_side_effects=True),
        name="exchange",
    )(row_dest, row_coarse, parent_vals, elevation, flux_x, flux_y, depth, depth, wet_mask,
      wet_mask, edge_owner.T, edge_panels, elevation, flux_x, flux_y, depth, wet_mask)

    width = cx + LANES
    rows = PAD + cy + STATE_HI
    ext_rows = rows + PAD
    win = cy + 2 * PAD
    return pl.pallas_call(
        functools.partial(step_kernel, ny, nx),
        out_shape=(sds((cy, cx), F32),) * 3,
        in_specs=[sm] + [any_] * 17,
        out_specs=(vm,) * 3,
        scratch_shapes=[
            pltpu.VMEM((3, ext_rows, width), F32),
            pltpu.VMEM((ext_rows, width), F32),
            pltpu.VMEM((STEPS, ext_rows, width), I32),
            pltpu.VMEM((rows, 2 * LANES), F32),
            pltpu.VMEM((rows, LANES), F32),
            pltpu.VMEM((3, nx, STEPS, cy), F32),
            pltpu.VMEM((9, STEPS, n_coarse, n_cols), F32),
            pltpu.VMEM((5, width // LANES, win + PAD, LANES), F32),
            pltpu.VMEM((3, win, width), F32),
            pltpu.VMEM((win, width), F32),
            pltpu.VMEM((2 * n_cols, width), BF16),
            pltpu.VMEM((3, width // LANES, win + PAD, LANES), F32),
            dma((32,)),
        ],
        compiler_params=pltpu.CompilerParams(vmem_limit_bytes=56 * 1024 * 1024),
        name="steps",
    )(shifts.T, elevation, flux_x, flux_y, depth, wet_mask, *halos)


def solution(mesh):
    in_specs = (
        P("ny", "nx"),
        P("ny", "nx"),
        P("ny", "nx"),
        P("ny", "nx"),
        P(None, "ny", "nx"),
        P(),
        P(None, ("ny", "nx"), None),
        P(None, ("ny", "nx")),
        P(None, ("ny", "nx")),
        P(None, "ny"),
        P(None, "nx", "ny"),
    )
    out_specs = (P("ny", "nx"), P("ny", "nx"), P("ny", "nx"))
    return jax.shard_map(local, mesh=mesh, in_specs=in_specs, out_specs=out_specs, check_vma=False)
```
